32 devices in a mesh: head: 2 (over y), seq: 8 (over z, x), rep: 2 (over core).
Axes of the slice: x: 2, y: 2, z: 4, core: 2. Of those that a mesh axis runs over, the one named last changes fastest.
Arguments:
- cache_keys: bfloat16 [8192, 4, 128], P(('rep', 'head', 'seq')), parts along dimension 0, may hold values from -6 to 6
- cache_values: bfloat16 [8192, 4, 128], P(('rep', 'head', 'seq')), parts along dimension 0, may hold values from -6 to 6
- span_slots: int32 [64], P('rep'), parts along dimension 0, may hold values from 0 to 31, each once
- prompt_length: int32 [2], P('rep'), parts along dimension 0, may hold values from 2048 to 4096
- queries: bfloat16 [32, 64, 128], P('rep', 'head'), parts along dimension 0, may hold values from -10 to 10
- new_keys: bfloat16 [32, 4, 128], P('rep', 'head'), parts along dimension 0, may hold values from -10 to 10
- new_values: bfloat16 [32, 4, 128], P('rep', 'head'), parts along dimension 0, may hold values from -6 to 6
- decode_offsets: int32 [32], P('rep'), parts along dimension 0, may hold values from 0 to 7
Outputs:
- relaid_keys: bfloat16 [8192, 4, 128], P(('rep', 'seq'), 'head'), parts along dimension 0
- relaid_values: bfloat16 [8192, 4, 128], P(('rep', 'seq'), 'head'), parts along dimension 0
- attended: bfloat16 [32, 64, 128], P('rep', 'head'), parts along dimension 0
The draws below stay inside these ranges and needn't reach their ends.
There are 2 independent parts, one for each index of `rep`. The reference program is written for one: setup_inputs(seed, part) draws one part's arguments, and reference() takes and returns one part's arrays. A program takes and returns all parts, laid end to end along the dimension named above; each array names one. Nothing has to cross between parts.
Inputs may be any that keep to these rules, and one draw needn't show every extreme that they name: span_slots names every slot of a round once.
All inputs are finite; a program needn't handle non-finite values.
Results may differ from the reference program's by a relative error of at most 0.0035.
Values may be sent and summed in bfloat16 or wider, within the bound.
No kernel may reach another device: no remote copies, remote signals or barrier semaphores. Data moves between devices by JAX's collectives and lax.ppermute only.
A program may use at most 64 MiB of HBM per device.

```python
import math
import jax
import jax.numpy as jnp
from jax import lax

KVH = 4
HD = 128
QH = 64
QTOK = 16
SEQ = 4096
SLOTS = 32
SPAN = 16
N_SEQ = 8


def draw_cache_keys(key, part):
    own_key = jax.random.fold_in(key, 11)
    values_drawn = jnp.clip(jax.random.normal(own_key, (SEQ, KVH, HD), jnp.float32), -6.0, 6.0)
    return values_drawn.astype(jnp.bfloat16)


def draw_queries(key, part):
    own_key = jax.random.fold_in(key, 23)
    values_drawn = jnp.clip(3.0 * jax.random.normal(own_key, (QTOK, QH, HD), jnp.float32), -10.0, 10.0)
    return values_drawn.astype(jnp.bfloat16)


def draw_new_keys(key, part):
    own_key = jax.random.fold_in(key, 37)
    values_drawn = jnp.clip(3.0 * jax.random.normal(own_key, (QTOK, KVH, HD), jnp.float32), -10.0, 10.0)
    return values_drawn.astype(jnp.bfloat16)


def place_ends(result, stream_key, low, high):
    longest = result.shape.index(max(result.shape))
    spots = []
    for shift in (0, 1):
        where = [jax.random.randint(jax.random.fold_in(stream_key, axis), (), 0, length) for axis, length in enumerate(result.shape)]
        where[longest] = (where[longest] + shift) % result.shape[longest]
        spots.append(tuple(where))
    return result.at[spots[0]].set(low).at[spots[1]].set(high)


def block_levels(key, extent, cuts, low, top_value):
    def one(axis_at, parts):
        draws = jax.random.uniform(jax.random.fold_in(jax.random.fold_in(key, 6), axis_at), (parts,), jnp.float32, low / len(cuts), top_value / len(cuts))
        return jnp.repeat(jnp.exp(draws), extent[axis_at] // parts).reshape((-1,) + (1,) * (len(extent) - axis_at - 1))

    level = one(*cuts[0])
    for cut in cuts[1:]:
        level = level * one(*cut)
    return level


def centred(key, extent, scale, bound, cuts=(), held_as=jnp.bfloat16):
    level = block_levels(key, extent, cuts, -0.22, 0.18) if cuts else 1.0
    values = jax.random.normal(key, extent, jnp.float32) * scale * level
    return jnp.minimum(jnp.maximum(values, -bound), bound).astype(held_as)


def setup_inputs(seed: int = 0, part: int = 0) -> dict:
    key_of = jax.random.split(jax.random.key(seed), 9)
    own_keys = jax.random.split(jax.random.fold_in(key_of[8], part), 9)
    cache_keys = draw_cache_keys(jax.random.fold_in(jax.random.fold_in(key_of[8], part), 71), part)
    cache_values = centred(own_keys[1], (SEQ, KVH, HD), 1.0, 6.0, ((0, 16),))
    span_slots = jax.random.permutation(own_keys[2], SLOTS).astype(jnp.int32)
    prompt_length = jax.random.randint(own_keys[3], (1,), SEQ // 2, SEQ + 1).astype(jnp.int32)
    queries = draw_queries(jax.random.fold_in(jax.random.fold_in(key_of[8], part), 71), part)
    new_keys = draw_new_keys(jax.random.fold_in(jax.random.fold_in(key_of[8], part), 71), part)
    new_values = centred(own_keys[6], (QTOK, KVH, HD), 1.0, 6.0, ((1, 2),))
    decode_offsets = place_ends(jax.random.randint(own_keys[7], (QTOK,), 0, QTOK // 2), jax.random.fold_in(own_keys[7], 1), 0, (QTOK // 2) - 1).astype(jnp.int32)
    return {"cache_keys": cache_keys, "cache_values": cache_values, "span_slots": span_slots, "prompt_length": prompt_length, "queries": queries, "new_keys": new_keys, "new_values": new_values, "decode_offsets": decode_offsets}


def relayout(stored, span_slots):
    cycle_size = SLOTS // 2
    blocks = stored.reshape(cycle_size, N_SEQ, 2, SPAN, KVH, HD)
    blocks = jnp.transpose(blocks, (1, 0, 2, 3, 4, 5)).reshape(N_SEQ, SLOTS, SPAN, KVH, HD)
    ordered = jnp.take(blocks, span_slots.astype(jnp.int32), axis=1)
    return ordered.reshape(SEQ, KVH, HD)

def reference(cache_keys, cache_values, span_slots, prompt_length, queries, new_keys, new_values, decode_offsets):
    length = prompt_length[0]
    positions = jnp.arange(SEQ, dtype=jnp.int32)
    live_rows = positions < length
    relaid_keys = jnp.where(live_rows[:, None, None], relayout(cache_keys, span_slots), jnp.zeros((), cache_keys.dtype))
    relaid_values = jnp.where(live_rows[:, None, None], relayout(cache_values, span_slots), jnp.zeros((), cache_values.dtype))
    group_size = QH // KVH
    score_scale = 1.0 / math.sqrt(HD)
    visible = decode_offsets[None, :] <= decode_offsets[:, None]
    row_visible = jnp.repeat(visible, group_size, axis=0)

    def per_head(head_index):
        query_block = lax.dynamic_slice_in_dim(queries, head_index * group_size, group_size, 1).reshape(QTOK * group_size, HD)
        key_block = jnp.take(relaid_keys, head_index, axis=1)
        value_block = jnp.take(relaid_values, head_index, axis=1)
        new_key_block = jnp.take(new_keys, head_index, axis=1)
        new_value_block = jnp.take(new_values, head_index, axis=1)
        cache_scores = jnp.dot(query_block, key_block.T, preferred_element_type=jnp.float32) * score_scale
        cache_scores = jnp.where(live_rows[None, :], cache_scores, -1e+30)
        new_scores = jnp.dot(query_block, new_key_block.T, preferred_element_type=jnp.float32) * score_scale
        new_scores = jnp.where(row_visible, new_scores, -1e+30)
        peak = jnp.maximum(lax.optimization_barrier(jnp.max(cache_scores, axis=1)), lax.optimization_barrier(jnp.max(new_scores, axis=1)))
        cache_weights = jnp.exp(cache_scores - peak[:, None])
        new_weights = jnp.exp(new_scores - peak[:, None])
        weight_total = lax.optimization_barrier(jnp.sum(cache_weights, axis=1)) + lax.optimization_barrier(jnp.sum(new_weights, axis=1))
        weighted = jnp.dot(cache_weights.astype(jnp.bfloat16), value_block, preferred_element_type=jnp.float32)
        weighted = weighted + jnp.dot(new_weights.astype(jnp.bfloat16), new_value_block, preferred_element_type=jnp.float32)
        return (weighted / weight_total[:, None]).reshape(QTOK, group_size, HD)
    outputs = lax.map(per_head, jnp.arange(KVH, dtype=jnp.int32))
    attended = jnp.transpose(outputs, (1, 0, 2, 3)).reshape(QTOK, QH, HD).astype(jnp.bfloat16)
    return (relaid_keys, relaid_values, attended)
```

```python
import functools
import math

import jax
import jax.numpy as jnp
from jax import lax
from jax.experimental import pallas as pl
from jax.experimental.pallas import tpu as pltpu
from jax.sharding import PartitionSpec as P

BF16 = jnp.bfloat16
F32 = jnp.float32
DEAD = -1e30
STAT_ROWS = 16
VMEM = pl.BlockSpec(memory_space=pltpu.VMEM)
SMEM = pl.BlockSpec(memory_space=pltpu.SMEM)
ANY = pl.BlockSpec(memory_space=pl.ANY)


def dot_rows(a, b):
    return lax.dot_general(a, b, (((1,), (1,)), ((), ())), preferred_element_type=F32)


def three_parts(x):
    high = x.astype(BF16).astype(F32)
    rest = x - high
    middle = rest.astype(BF16).astype(F32)
    return high, middle, rest - middle


def pack_kernel(keys_ref, values_ref, send_ref, held, in_sems, out_sems):
    head_count = keys_ref.shape[2]
    pieces = [(c, h) for h in range(head_count) for c in range(2)]
    ins = []
    for c, h in pieces:
        source = (keys_ref, values_ref)[c]
        copy = pltpu.make_async_copy(source.at[:, :, h], held.at[c, h], in_sems.at[c, h])
        copy.start()
        ins.append(copy)
    outs = []
    for (c, h), copy in zip(pieces, ins):
        copy.wait()
        out = pltpu.make_async_copy(held.at[c, h], send_ref.at[h, :, c], out_sems.at[c, h])
        out.start()
        outs.append(out)
    for out in outs:
        out.wait()


def pack(cache_keys, cache_values, seq_count, head_count):
    row_count, kv_all, head_dim = cache_keys.shape
    split = (seq_count, row_count // seq_count, head_count, kv_all // head_count, head_dim)
    rows, kv = split[1], split[3]
    return pl.pallas_call(
        pack_kernel,
        out_shape=jax.ShapeDtypeStruct((head_count, seq_count, 2, rows, kv, head_dim), BF16),
        in_specs=[ANY, ANY],
        out_specs=ANY,
        scratch_shapes=[
            pltpu.VMEM((2, head_count, seq_count, rows, kv, head_dim), BF16),
            pltpu.SemaphoreType.DMA((2, head_count)),
            pltpu.SemaphoreType.DMA((2, head_count)),
        ],
        name="pack",
    )(cache_keys.reshape(split), cache_values.reshape(split))


def partial_kernel(score_scale, seq_count, query_ref, got_ref, bias_ref, out_ref, rows_buf, stat_buf):
    tokens, heads, head_dim = query_ref.shape
    kv_count = bias_ref.shape[0]
    columns = bias_ref.shape[1]
    group = heads // kv_count
    keys = got_ref[:, 0].reshape(columns, head_dim)
    values = got_ref[:, 1].reshape(columns, head_dim)
    lane = lax.broadcasted_iota(jnp.int32, (tokens * group, head_dim), 1)
    for g in range(kv_count):
        query = query_ref[:, g * group : (g + 1) * group, :].reshape(tokens * group, head_dim)
        scores = dot_rows(query, keys) * score_scale + bias_ref[g : g + 1, :]
        peak = jnp.max(scores, axis=1, keepdims=True)
        weights = jnp.exp(scores - peak)
        total = jnp.sum(weights, axis=1, keepdims=True)
        weighted = jnp.dot(weights.astype(BF16), values, preferred_element_type=F32)
        stats = jnp.zeros((tokens * group, head_dim), F32)
        for at, part in enumerate(three_parts(peak) + three_parts(total)):
            stats = jnp.where(lane == at, part, stats)
        rows_buf[:, g] = weighted.astype(BF16).reshape(tokens, group, head_dim)
        stat_buf[:, g] = stats.astype(BF16).reshape(tokens, group, head_dim)
    per = tokens * heads // seq_count
    all_rows = rows_buf[...].reshape(tokens * heads, head_dim)
    all_stats = stat_buf[...].reshape(tokens * heads, head_dim)
    pick = (
        lax.broadcasted_iota(jnp.int32, (STAT_ROWS, head_dim), 0)
        == lax.broadcasted_iota(jnp.int32, (STAT_ROWS, head_dim), 1)
    ).astype(F32).astype(BF16)
    turned = dot_rows(pick, all_stats).astype(BF16)
    for s in range(seq_count):
        out_ref[s, :per, :] = all_rows[s * per : (s + 1) * per]
        out_ref[s, per:, :per] = turned[:, s * per : (s + 1) * per]


def partial_rows(query, got, bias, score_scale, seq_count):
    tokens, heads, head_dim = query.shape
    kv_count = bias.shape[0]
    group = heads // kv_count
    per = tokens * heads // seq_count
    return pl.pallas_call(
        functools.partial(partial_kernel, score_scale, seq_count),
        out_shape=jax.ShapeDtypeStruct((seq_count, per + STAT_ROWS, head_dim), BF16),
        in_specs=[VMEM, VMEM, VMEM],
        out_specs=VMEM,
        scratch_shapes=[
            pltpu.VMEM((tokens, kv_count, group, head_dim), BF16),
            pltpu.VMEM((tokens, kv_count, group, head_dim), BF16),
        ],
        name="partial_rows",
    )(query, got, bias)


def new_kernel(score_scale, query_ref, keys_ref, values_ref, bias_ref, weighted_ref, peak_ref, total_ref):
    scores = dot_rows(query_ref[...], keys_ref[...]) * score_scale + bias_ref[...]
    peak = jnp.max(scores, axis=1, keepdims=True)
    weights = jnp.exp(scores - peak)
    total = jnp.sum(weights, axis=1, keepdims=True)
    weighted_ref[...] = jnp.dot(
        weights.astype(BF16), values_ref[...], preferred_element_type=F32
    )
    peak_ref[...] = jnp.broadcast_to(peak, peak_ref.shape)
    total_ref[...] = jnp.broadcast_to(total, total_ref.shape)


def new_rows(query, keys, values, bias, score_scale):
    shape = jax.ShapeDtypeStruct(query.shape, F32)
    return pl.pallas_call(
        functools.partial(new_kernel, score_scale),
        out_shape=(shape, shape, shape),
        in_specs=[VMEM] * 4,
        out_specs=(VMEM, VMEM, VMEM),
        name="new_rows",
    )(query, keys, values, bias)


def merge_kernel(got_ref, weighted_ref, peak_ref, total_ref, out_ref):
    seq_count = got_ref.shape[0]
    per, head_dim = weighted_ref.shape
    eye = (
        lax.broadcasted_iota(jnp.int32, (per, per), 0)
        == lax.broadcasted_iota(jnp.int32, (per, per), 1)
    ).astype(F32).astype(BF16)
    stats = got_ref[:, per:, :per].reshape(seq_count * STAT_ROWS, per)
    turned = dot_rows(eye, stats)

    def column(s, at):
        base = s * STAT_ROWS + at
        parts = [turned[:, base + k : base + k + 1] for k in range(3)]
        return jnp.broadcast_to(parts[0] + parts[1] + parts[2], (per, head_dim))

    peaks = [column(s, 0) for s in range(seq_count)] + [peak_ref[...]]
    peak = functools.reduce(jnp.maximum, peaks)
    scale = jnp.exp(peaks[-1] - peak)
    total = total_ref[...] * scale
    weighted = weighted_ref[...] * scale
    for s in range(seq_count):
        scale = jnp.exp(peaks[s] - peak)
        total = total + column(s, 3) * scale
        weighted = weighted + got_ref[s, :per, :].astype(F32) * scale
    result = (weighted / total).astype(BF16)
    for s in range(seq_count):
        out_ref[s] = result


def merge(got, weighted, peak, total):
    seq_count = got.shape[0]
    return pl.pallas_call(
        merge_kernel,
        out_shape=jax.ShapeDtypeStruct((seq_count,) + weighted.shape, BF16),
        in_specs=[VMEM] * 4,
        out_specs=VMEM,
        name="merge",
    )(got, weighted, peak, total)


def relay_kernel(slots_ref, live_ref, got_ref, keys_ref, values_ref):
    slot_count, span, head_dim = keys_ref.shape
    row = lax.broadcasted_iota(jnp.int32, (span, head_dim), 0)
    live = live_ref[0]

    def one(t, carry):
        slot = slots_ref[t]
        kept = row < live - t * span
        for c, out_ref in enumerate((keys_ref, values_ref)):
            block = got_ref[slot // 2, c, slot % 2].astype(F32)
            out_ref[t] = jnp.where(kept, block, 0.0).astype(BF16)
        return carry

    lax.fori_loop(0, slot_count, one, 0, unroll=4)


def relay(span_slots, live, got):
    cycle, _, _, span, head_dim = got.shape
    shape = jax.ShapeDtypeStruct((span_slots.shape[0], span, head_dim), BF16)
    return pl.pallas_call(
        relay_kernel,
        out_shape=(shape, shape),
        in_specs=[SMEM, SMEM, VMEM],
        out_specs=(VMEM, VMEM),
        name="relay",
    )(span_slots, live, got)


def body(
    cache_keys,
    cache_values,
    span_slots,
    prompt_length,
    queries,
    new_keys,
    new_values,
    decode_offsets,
):
    row_count, kv_all, head_dim = cache_keys.shape
    seq_count = lax.axis_size("seq")
    head_count = lax.axis_size("head")
    cycle_size = seq_count * head_count
    slot_count = span_slots.shape[0]
    span_rows = row_count // (2 * seq_count)
    kv_local = kv_all // head_count
    token_count, heads, _ = queries.shape
    group_size = heads // kv_local
    length = prompt_length[0]
    score_scale = 1.0 / math.sqrt(head_dim)
    shard_rows = slot_count * span_rows
    seq_index = lax.axis_index("seq")
    shard_start = seq_index * shard_rows

    packed = pack(cache_keys, cache_values, seq_count, head_count)
    got = lax.all_to_all(
        packed.reshape(cycle_size, 2, 2 * span_rows * kv_local, head_dim),
        ("head", "seq"),
        split_axis=0,
        concat_axis=0,
        tiled=True,
    )

    spans = jnp.arange(slot_count, dtype=jnp.int32)
    place = jnp.sum(
        jnp.where(span_slots[None, :] == spans[:, None], spans[None, :], 0), axis=1
    )
    column = jnp.arange(shard_rows * kv_local, dtype=jnp.int32)
    position = (
        jnp.broadcast_to(
            (place * span_rows)[:, None], (slot_count, span_rows * kv_local)
        ).reshape(-1)
        + (column // kv_local) % span_rows
        + shard_start
    )
    matches = (column % kv_local)[None, :] == jnp.arange(kv_local, dtype=jnp.int32)[:, None]
    bias = jnp.where(matches & (position < length)[None, :], 0.0, DEAD).astype(F32)

    per = token_count * heads // seq_count
    own_row = seq_index * per + jnp.arange(per, dtype=jnp.int32)
    own_token = own_row // heads
    own_kv = (own_row // group_size) % kv_local
    own_query = lax.dynamic_slice_in_dim(
        queries.reshape(token_count * heads, head_dim), seq_index * per, per, 0
    )
    new_column = jnp.arange(token_count * kv_local, dtype=jnp.int32)
    own_offset = jnp.sum(
        jnp.where(
            own_token[:, None] == jnp.arange(token_count, dtype=jnp.int32)[None, :],
            decode_offsets[None, :],
            0,
        ),
        axis=1,
    )
    visible = jnp.repeat(decode_offsets, kv_local)[None, :] <= own_offset[:, None]
    visible = visible & ((new_column % kv_local)[None, :] == own_kv[:, None])
    new_bias = jnp.where(visible, 0.0, DEAD).astype(F32)
    fresh = new_rows(
        own_query,
        new_keys.reshape(token_count * kv_local, head_dim),
        new_values.reshape(token_count * kv_local, head_dim),
        new_bias,
        score_scale,
    )

    partial = partial_rows(queries, got, bias, score_scale, seq_count)
    shares = lax.all_to_all(partial, "seq", split_axis=0, concat_axis=0, tiled=True)
    merged = merge(shares, *fresh)
    attended = lax.all_to_all(merged, "seq", split_axis=0, concat_axis=0, tiled=True)

    live = jnp.clip(length - shard_start, 0, shard_rows) * kv_local
    relaid_keys, relaid_values = relay(
        span_slots,
        live.reshape(1),
        got.reshape(cycle_size, 2, 2, span_rows * kv_local, head_dim),
    )
    whole = (shard_rows, kv_local, head_dim)
    return (
        relaid_keys.reshape(whole),
        relaid_values.reshape(whole),
        attended.reshape(token_count, heads, head_dim),
    )


def solution(mesh):
    return jax.shard_map(
        body,
        mesh=mesh,
        in_specs=(
            P(("rep", "head", "seq"), None, None),
            P(("rep", "head", "seq"), None, None),
            P("rep"),
            P("rep"),
            P("rep", "head", None),
            P("rep", "head", None),
            P("rep", "head", None),
            P("rep"),
        ),
        out_specs=(
            P(("rep", "seq"), "head", None),
            P(("rep", "seq"), "head", None),
            P("rep", "head", None),
        ),
        check_vma=False,
    )
```

```python
import functools
import math

import jax
import jax.numpy as jnp
from jax import lax
from jax.experimental import pallas as pl
from jax.experimental.pallas import tpu as pltpu
from jax.sharding import PartitionSpec as P

BF16 = jnp.bfloat16
F32 = jnp.float32
DEAD = -1e30
STAT_ROWS = 16
VMEM = pl.BlockSpec(memory_space=pltpu.VMEM)
SMEM = pl.BlockSpec(memory_space=pltpu.SMEM)
ANY = pl.BlockSpec(memory_space=pl.ANY)
PARAMS = pltpu.CompilerParams(vmem_limit_bytes=16 * 1024 * 1024)


def dot_rows(a, b):
    return lax.dot_general(a, b, (((1,), (1,)), ((), ())), preferred_element_type=F32)


def three_parts(x):
    high = x.astype(BF16).astype(F32)
    rest = x - high
    middle = rest.astype(BF16).astype(F32)
    return high, middle, rest - middle


def pack_kernel(keys_ref, values_ref, send_ref, sems):
    copies = []
    for h in range(keys_ref.shape[2]):
        for c, source in enumerate((keys_ref, values_ref)):
            copy = pltpu.make_async_copy(
                source.at[:, :, h], send_ref.at[h, :, c], sems.at[c, h]
            )
            copy.start()
            copies.append(copy)
    for copy in copies:
        copy.wait()


def pack(cache_keys, cache_values, seq_count, head_count):
    row_count, kv_all, head_dim = cache_keys.shape
    split = (seq_count, row_count // seq_count, head_count, kv_all // head_count, head_dim)
    rows, kv = split[1], split[3]
    return pl.pallas_call(
        pack_kernel,
        out_shape=jax.ShapeDtypeStruct((head_count, seq_count, 2, rows, kv, head_dim), BF16),
        in_specs=[VMEM, VMEM],
        out_specs=ANY,
        scratch_shapes=[pltpu.SemaphoreType.DMA((2, head_count))],
        compiler_params=PARAMS,
        name="pack",
    )(cache_keys.reshape(split), cache_values.reshape(split))


def partial_kernel(score_scale, seq_count, query_ref, got_ref, bias_ref, out_ref, rows_buf, stat_buf):
    tokens, heads, head_dim = query_ref.shape
    kv_count = bias_ref.shape[0]
    columns = bias_ref.shape[1]
    group = heads // kv_count
    keys = got_ref[:, 0].reshape(columns, head_dim)
    values = got_ref[:, 1].reshape(columns, head_dim)
    lane = lax.broadcasted_iota(jnp.int32, (tokens * group, head_dim), 1)
    for g in range(kv_count):
        query = query_ref[:, g * group : (g + 1) * group, :].reshape(tokens * group, head_dim)
        scores = dot_rows(query, keys) * score_scale + bias_ref[g : g + 1, :]
        peak = jnp.max(scores, axis=1, keepdims=True)
        weights = jnp.exp(scores - peak)
        total = jnp.sum(weights, axis=1, keepdims=True)
        weighted = jnp.dot(weights.astype(BF16), values, preferred_element_type=F32)
        stats = jnp.zeros((tokens * group, head_dim), F32)
        for at, part in enumerate(three_parts(peak) + three_parts(total)):
            stats = jnp.where(lane == at, part, stats)
        rows_buf[:, g] = weighted.astype(BF16).reshape(tokens, group, head_dim)
        stat_buf[:, g] = stats.astype(BF16).reshape(tokens, group, head_dim)
    per = tokens * heads // seq_count
    all_rows = rows_buf[...].reshape(tokens * heads, head_dim)
    all_stats = stat_buf[...].reshape(tokens * heads, head_dim)
    pick = (
        lax.broadcasted_iota(jnp.int32, (STAT_ROWS, head_dim), 0)
        == lax.broadcasted_iota(jnp.int32, (STAT_ROWS, head_dim), 1)
    ).astype(F32).astype(BF16)
    turned = dot_rows(pick, all_stats).astype(BF16)
    for s in range(seq_count):
        out_ref[s, :per, :] = all_rows[s * per : (s + 1) * per]
        out_ref[s, per:, :per] = turned[:, s * per : (s + 1) * per]


def partial_rows(query, got, bias, score_scale, seq_count):
    tokens, heads, head_dim = query.shape
    kv_count = bias.shape[0]
    group = heads // kv_count
    per = tokens * heads // seq_count
    return pl.pallas_call(
        functools.partial(partial_kernel, score_scale, seq_count),
        out_shape=jax.ShapeDtypeStruct((seq_count, per + STAT_ROWS, head_dim), BF16),
        in_specs=[VMEM, VMEM, VMEM],
        out_specs=VMEM,
        scratch_shapes=[
            pltpu.VMEM((tokens, kv_count, group, head_dim), BF16),
            pltpu.VMEM((tokens, kv_count, group, head_dim), BF16),
        ],
        compiler_params=PARAMS,
        name="partial_rows",
    )(query, got, bias)


def new_kernel(score_scale, query_ref, keys_ref, values_ref, bias_ref, weighted_ref, peak_ref, total_ref):
    scores = dot_rows(query_ref[...], keys_ref[...]) * score_scale + bias_ref[...]
    peak = jnp.max(scores, axis=1, keepdims=True)
    weights = jnp.exp(scores - peak)
    total = jnp.sum(weights, axis=1, keepdims=True)
    weighted_ref[...] = jnp.dot(
        weights.astype(BF16), values_ref[...], preferred_element_type=F32
    )
    peak_ref[...] = jnp.broadcast_to(peak, peak_ref.shape)
    total_ref[...] = jnp.broadcast_to(total, total_ref.shape)


def new_rows(query, keys, values, bias, score_scale):
    shape = jax.ShapeDtypeStruct(query.shape, F32)
    return pl.pallas_call(
        functools.partial(new_kernel, score_scale),
        out_shape=(shape, shape, shape),
        in_specs=[VMEM] * 4,
        out_specs=(VMEM, VMEM, VMEM),
        compiler_params=PARAMS,
        name="new_rows",
    )(query, keys, values, bias)


def merge_kernel(got_ref, weighted_ref, peak_ref, total_ref, out_ref):
    seq_count = got_ref.shape[0]
    per, head_dim = weighted_ref.shape
    eye = (
        lax.broadcasted_iota(jnp.int32, (per, per), 0)
        == lax.broadcasted_iota(jnp.int32, (per, per), 1)
    ).astype(F32).astype(BF16)
    stats = got_ref[:, per:, :per].reshape(seq_count * STAT_ROWS, per)
    turned = dot_rows(eye, stats)

    def column(s, at):
        base = s * STAT_ROWS + at
        parts = [turned[:, base + k : base + k + 1] for k in range(3)]
        return jnp.broadcast_to(parts[0] + parts[1] + parts[2], (per, head_dim))

    peaks = [column(s, 0) for s in range(seq_count)] + [peak_ref[...]]
    peak = functools.reduce(jnp.maximum, peaks)
    scale = jnp.exp(peaks[-1] - peak)
    total = total_ref[...] * scale
    weighted = weighted_ref[...] * scale
    for s in range(seq_count):
        scale = jnp.exp(peaks[s] - peak)
        total = total + column(s, 3) * scale
        weighted = weighted + got_ref[s, :per, :].astype(F32) * scale
    result = (weighted / total).astype(BF16)
    for s in range(seq_count):
        out_ref[s] = result


def merge(got, weighted, peak, total):
    seq_count = got.shape[0]
    return pl.pallas_call(
        merge_kernel,
        out_shape=jax.ShapeDtypeStruct((seq_count,) + weighted.shape, BF16),
        in_specs=[VMEM] * 4,
        out_specs=VMEM,
        compiler_params=PARAMS,
        name="merge",
    )(got, weighted, peak, total)


def relay_kernel(slots_ref, live_ref, got_ref, keys_ref, values_ref):
    slot_count, span, head_dim = keys_ref.shape
    row = lax.broadcasted_iota(jnp.int32, (span, head_dim), 0)
    live = live_ref[0]

    def one(t, carry):
        slot = slots_ref[t]
        kept = row < live - t * span
        for c, out_ref in enumerate((keys_ref, values_ref)):
            block = got_ref[slot // 2, c, slot % 2].astype(F32)
            out_ref[t] = jnp.where(kept, block, 0.0).astype(BF16)
        return carry

    lax.fori_loop(0, slot_count, one, 0, unroll=4)


def relay(span_slots, live, got):
    cycle, _, _, span, head_dim = got.shape
    shape = jax.ShapeDtypeStruct((span_slots.shape[0], span, head_dim), BF16)
    return pl.pallas_call(
        relay_kernel,
        out_shape=(shape, shape),
        in_specs=[SMEM, SMEM, VMEM],
        out_specs=(VMEM, VMEM),
        compiler_params=PARAMS,
        name="relay",
    )(span_slots, live, got)


def body(
    cache_keys,
    cache_values,
    span_slots,
    prompt_length,
    queries,
    new_keys,
    new_values,
    decode_offsets,
):
    row_count, kv_all, head_dim = cache_keys.shape
    seq_count = lax.axis_size("seq")
    head_count = lax.axis_size("head")
    cycle_size = seq_count * head_count
    slot_count = span_slots.shape[0]
    span_rows = row_count // (2 * seq_count)
    kv_local = kv_all // head_count
    token_count, heads, _ = queries.shape
    group_size = heads // kv_local
    length = prompt_length[0]
    score_scale = 1.0 / math.sqrt(head_dim)
    shard_rows = slot_count * span_rows
    seq_index = lax.axis_index("seq")
    shard_start = seq_index * shard_rows

    packed = pack(cache_keys, cache_values, seq_count, head_count)
    got = lax.all_to_all(
        packed.reshape(cycle_size, 2, 2 * span_rows * kv_local, head_dim),
        ("head", "seq"),
        split_axis=0,
        concat_axis=0,
        tiled=True,
    )

    spans = jnp.arange(slot_count, dtype=jnp.int32)
    place = jnp.sum(
        jnp.where(span_slots[None, :] == spans[:, None], spans[None, :], 0), axis=1
    )
    column = jnp.arange(shard_rows * kv_local, dtype=jnp.int32)
    position = (
        jnp.broadcast_to(
            (place * span_rows)[:, None], (slot_count, span_rows * kv_local)
        ).reshape(-1)
        + (column // kv_local) % span_rows
        + shard_start
    )
    matches = (column % kv_local)[None, :] == jnp.arange(kv_local, dtype=jnp.int32)[:, None]
    bias = jnp.where(matches & (position < length)[None, :], 0.0, DEAD).astype(F32)

    per = token_count * heads // seq_count
    own_row = seq_index * per + jnp.arange(per, dtype=jnp.int32)
    own_token = own_row // heads
    own_kv = (own_row // group_size) % kv_local
    own_query = lax.dynamic_slice_in_dim(
        queries.reshape(token_count * heads, head_dim), seq_index * per, per, 0
    )
    new_column = jnp.arange(token_count * kv_local, dtype=jnp.int32)
    own_offset = jnp.sum(
        jnp.where(
            own_token[:, None] == jnp.arange(token_count, dtype=jnp.int32)[None, :],
            decode_offsets[None, :],
            0,
        ),
        axis=1,
    )
    visible = jnp.repeat(decode_offsets, kv_local)[None, :] <= own_offset[:, None]
    visible = visible & ((new_column % kv_local)[None, :] == own_kv[:, None])
    new_bias = jnp.where(visible, 0.0, DEAD).astype(F32)
    fresh = new_rows(
        own_query,
        new_keys.reshape(token_count * kv_local, head_dim),
        new_values.reshape(token_count * kv_local, head_dim),
        new_bias,
        score_scale,
    )

    partial = partial_rows(queries, got, bias, score_scale, seq_count)
    shares = lax.all_to_all(partial, "seq", split_axis=0, concat_axis=0, tiled=True)
    merged = merge(shares, *fresh)
    attended = lax.all_to_all(merged, "seq", split_axis=0, concat_axis=0, tiled=True)

    live = jnp.clip(length - shard_start, 0, shard_rows) * kv_local
    relaid_keys, relaid_values = relay(
        span_slots,
        live.reshape(1),
        got.reshape(cycle_size, 2, 2, span_rows * kv_local, head_dim),
    )
    whole = (shard_rows, kv_local, head_dim)
    return (
        relaid_keys.reshape(whole),
        relaid_values.reshape(whole),
        attended.reshape(token_count, heads, head_dim),
    )


def solution(mesh):
    return jax.shard_map(
        body,
        mesh=mesh,
        in_specs=(
            P(("rep", "head", "seq"), None, None),
            P(("rep", "head", "seq"), None, None),
            P("rep"),
            P("rep"),
            P("rep", "head", None),
            P("rep", "head", None),
            P("rep", "head", None),
            P("rep"),
        ),
        out_specs=(
            P(("rep", "seq"), "head", None),
            P(("rep", "seq"), "head", None),
            P("rep", "head", None),
        ),
        check_vma=False,
    )
```

```python
import functools
import math

import jax
import jax.numpy as jnp
from jax import lax
from jax.experimental import pallas as pl
from jax.experimental.pallas import tpu as pltpu
from jax.sharding import PartitionSpec as P


BF16 = jnp.bfloat16
F32 = jnp.float32
DEAD = -1e30
STAT_ROWS = 16
LANES = 128
VMEM = pl.BlockSpec(memory_space=pltpu.VMEM)
SMEM = pl.BlockSpec(memory_space=pltpu.SMEM)
HBM = pl.BlockSpec(memory_space=pltpu.HBM)
PARAMS = pltpu.CompilerParams(vmem_limit_bytes=16 * 1024 * 1024)


def dot_rows(a, b):
    return lax.dot_general(a, b, (((1,), (1,)), ((), ())), preferred_element_type=F32)


def three_parts(x):
    high = x.astype(BF16).astype(F32)
    rest = x - high
    middle = rest.astype(BF16).astype(F32)
    return [high, middle, rest - middle]


def stacked(parts, like):
    row = lax.broadcasted_iota(jnp.int32, like, 0)
    out = jnp.zeros(like, F32)
    for at, part in enumerate(parts):
        out = jnp.where(row == at, part, out)
    return out.astype(BF16)


def eye(rows, columns):
    return (
        lax.broadcasted_iota(jnp.int32, (rows, columns), 0)
        == lax.broadcasted_iota(jnp.int32, (rows, columns), 1)
    ).astype(F32).astype(BF16)


def pack_kernel(head_index_ref, keys_ref, values_ref, send_ref, mine_ref, away_ref, held, in_sems, out_sems, mine_sems, away_sems):
    head_count = keys_ref.shape[2]
    me = head_index_ref[0]
    ins = {}
    for shift in list(range(1, head_count)) + [0]:
        h = lax.rem(me + shift, head_count)
        for c, source in enumerate((keys_ref, values_ref)):
            copy = pltpu.make_async_copy(source.at[:, :, h], held.at[shift, c], in_sems.at[shift, c])
            copy.start()
            ins[shift, c] = copy
    outs = []
    for (shift, c), copy in ins.items():
        copy.wait()
        h = lax.rem(me + shift, head_count)
        block = held.at[shift, c]
        if shift:
            outs.append(pltpu.make_async_copy(block, away_ref.at[shift - 1, c], away_sems.at[shift - 1, c]))
        else:
            outs.append(pltpu.make_async_copy(block, mine_ref.at[c], mine_sems.at[c]))
        outs[-1].start()
        outs.append(pltpu.make_async_copy(block, send_ref.at[h, :, c], out_sems.at[shift, c]))
        outs[-1].start()
    for out in outs:
        out.wait()


def pack(head_index, cache_keys, cache_values, seq_count, head_count):
    row_count, kv_all, head_dim = cache_keys.shape
    split = (seq_count, row_count // seq_count, head_count, kv_all // head_count, head_dim)
    rows, kv = split[1], split[3]
    block = (seq_count, rows, kv, head_dim)
    return pl.pallas_call(
        pack_kernel,
        out_shape=(
            jax.ShapeDtypeStruct((head_count, seq_count, 2, rows, kv, head_dim), BF16),
            jax.ShapeDtypeStruct((2,) + block, BF16),
            jax.ShapeDtypeStruct((head_count - 1, 2) + block, BF16),
        ),
        in_specs=[SMEM, HBM, HBM],
        out_specs=(HBM, VMEM, HBM),
        scratch_shapes=[
            pltpu.VMEM((head_count, 2) + block, BF16),
            pltpu.SemaphoreType.DMA((head_count, 2)),
            pltpu.SemaphoreType.DMA((head_count, 2)),
            pltpu.SemaphoreType.DMA((2,)),
            pltpu.SemaphoreType.DMA((head_count - 1, 2)),
        ],
        name="pack",
    )(head_index, cache_keys.reshape(split), cache_values.reshape(split))


def attend_kernel(score_scale, query_ref, new_keys_ref, new_values_ref, new_bias_ref, bias_ref, *rest):
    *block_refs, out_ref, rows_buf, stat_buf = rest
    tokens, heads, head_dim = query_ref.shape
    kv_count = bias_ref.shape[0]
    group = heads // kv_count
    lane = lax.broadcasted_iota(jnp.int32, (tokens * group, head_dim), 1)
    keys = jnp.concatenate([ref[0] for ref in block_refs], axis=0)
    values = jnp.concatenate([ref[1] for ref in block_refs], axis=0)
    for g in range(kv_count):
        query = query_ref[:, g * group : (g + 1) * group, :].reshape(tokens * group, head_dim)
        scores = dot_rows(query, keys) * score_scale + bias_ref[g : g + 1, :]
        fresh = dot_rows(query, new_keys_ref[...]) * score_scale + new_bias_ref[g]
        peak = jnp.maximum(
            jnp.max(scores, axis=1, keepdims=True), jnp.max(fresh, axis=1, keepdims=True)
        )
        weights = jnp.exp(scores - peak)
        fresh = jnp.exp(fresh - peak)
        total = jnp.sum(weights, axis=1, keepdims=True) + jnp.sum(fresh, axis=1, keepdims=True)
        weighted = jnp.dot(weights.astype(BF16), values, preferred_element_type=F32)
        weighted = weighted + jnp.dot(
            fresh.astype(BF16), new_values_ref[...], preferred_element_type=F32
        )
        stats = jnp.zeros((tokens * group, head_dim), F32)
        for at, part in enumerate(three_parts(peak) + three_parts(total)):
            stats = jnp.where(lane == at, part, stats)
        rows_buf[:, g] = weighted.astype(BF16).reshape(tokens, group, head_dim)
        stat_buf[:, g] = stats.astype(BF16).reshape(tokens, group, head_dim)
    count = tokens * heads
    out_ref[:count, :] = rows_buf[...].reshape(count, head_dim)
    turned = dot_rows(eye(STAT_ROWS, head_dim), stat_buf[...].reshape(count, head_dim))
    for at in range(count // LANES):
        start = count + at * STAT_ROWS
        out_ref[start : start + STAT_ROWS, :] = turned[:, at * LANES : (at + 1) * LANES].astype(BF16)


def attend(query, new_keys, new_values, new_bias, bias, blocks, score_scale):
    tokens, heads, head_dim = query.shape
    kv_count = bias.shape[0]
    group = heads // kv_count
    count = tokens * heads
    return pl.pallas_call(
        functools.partial(attend_kernel, score_scale),
        out_shape=jax.ShapeDtypeStruct((count + count // LANES * STAT_ROWS, head_dim), BF16),
        in_specs=[VMEM] * (5 + len(blocks)),
        out_specs=VMEM,
        scratch_shapes=[
            pltpu.VMEM((tokens, kv_count, group, head_dim), BF16),
            pltpu.VMEM((tokens, kv_count, group, head_dim), BF16),
        ],
        compiler_params=PARAMS,
        name="attend",
    )(query, new_keys, new_values, new_bias, bias, *blocks)


def merge_kernel(last, one_ref, two_ref, out_ref):
    head_dim = one_ref.shape[1]
    count = one_ref.shape[0] * LANES // (LANES + STAT_ROWS)
    turn = eye(LANES, LANES)
    for at in range(count // LANES):
        start = count + at * STAT_ROWS
        peaks, totals = [], []
        for ref in (one_ref, two_ref):
            stats = ref[start : start + STAT_ROWS, :].astype(F32)
            peaks.append(stats[0:1] + stats[1:2] + stats[2:3])
            totals.append(stats[3:4] + stats[4:5] + stats[5:6])
        peak = jnp.maximum(*peaks)
        factors = [jnp.exp(p - peak) for p in peaks]
        total = factors[0] * totals[0] + factors[1] * totals[1]
        if last:
            factors = [f / total for f in factors]
        else:
            out_ref[start : start + STAT_ROWS, :] = stacked(
                three_parts(peak) + three_parts(total), (STAT_ROWS, LANES)
            )
        columns = dot_rows(
            turn, stacked(three_parts(factors[0]) + three_parts(factors[1]), (STAT_ROWS, LANES))
        )
        result = None
        for k, ref in enumerate((one_ref, two_ref)):
            column = columns[:, 3 * k : 3 * k + 1] + columns[:, 3 * k + 1 : 3 * k + 2]
            column = jnp.broadcast_to(column + columns[:, 3 * k + 2 : 3 * k + 3], (LANES, head_dim))
            term = ref[at * LANES : (at + 1) * LANES, :].astype(F32) * column
            result = term if result is None else result + term
        out_ref[at * LANES : (at + 1) * LANES, :] = result.astype(BF16)


def merge(one, two, last):
    rows, head_dim = one.shape
    if last:
        rows = rows * LANES // (LANES + STAT_ROWS)
    return pl.pallas_call(
        functools.partial(merge_kernel, last),
        out_shape=jax.ShapeDtypeStruct((rows, head_dim), BF16),
        in_specs=[VMEM, VMEM],
        out_specs=VMEM,
        compiler_params=PARAMS,
        name="merge",
    )(one, two)


def relay_kernel(slots_ref, live_ref, got_ref, keys_ref, values_ref):
    slot_count, span, head_dim = keys_ref.shape
    row = lax.broadcasted_iota(jnp.int32, (span, head_dim), 0)
    live = live_ref[0]

    def one(t, carry):
        slot = slots_ref[t]
        kept = row < live - t * span
        for c, out_ref in enumerate((keys_ref, values_ref)):
            block = got_ref[slot // 2, c, slot % 2].astype(F32)
            out_ref[t] = jnp.where(kept, block, 0.0).astype(BF16)
        return carry

    lax.fori_loop(0, slot_count, one, 0, unroll=4)


def relay(span_slots, live, got):
    _, _, _, span, head_dim = got.shape
    shape = jax.ShapeDtypeStruct((span_slots.shape[0], span, head_dim), BF16)
    return pl.pallas_call(
        relay_kernel,
        out_shape=(shape, shape),
        in_specs=[SMEM, SMEM, VMEM],
        out_specs=(VMEM, VMEM),
        compiler_params=PARAMS,
        name="relay",
    )(span_slots, live, got)


def step(
    cache_keys,
    cache_values,
    span_slots,
    prompt_length,
    queries,
    new_keys,
    new_values,
    decode_offsets,
):
    row_count, kv_all, head_dim = cache_keys.shape
    seq_count = lax.axis_size("seq")
    head_count = lax.axis_size("head")
    cycle_size = seq_count * head_count
    slot_count = span_slots.shape[0]
    span_rows = row_count // (2 * seq_count)
    kv_local = kv_all // head_count
    token_count, heads, _ = queries.shape
    group_size = heads // kv_local
    length = prompt_length[0]
    score_scale = 1.0 / math.sqrt(head_dim)
    shard_rows = slot_count * span_rows
    seq_index = lax.axis_index("seq")
    head_index = lax.axis_index("head")
    shard_start = seq_index * shard_rows

    packed, mine, away = pack(
        head_index.reshape(1), cache_keys, cache_values, seq_count, head_count
    )
    flat = (2, row_count * kv_local, head_dim)
    blocks = [mine.reshape(flat)]
    for shift in range(1, head_count):
        blocks.append(
            lax.ppermute(
                away[shift - 1].reshape(flat),
                "head",
                [(h, (h + shift) % head_count) for h in range(head_count)],
            )
        )
    got = lax.all_to_all(
        packed.reshape(cycle_size, 2, 2 * span_rows * kv_local, head_dim),
        ("head", "seq"),
        split_axis=0,
        concat_axis=0,
        tiled=True,
    )

    columns = (head_count, seq_count, 2, span_rows, kv_local)

    def index_of(axis):
        return lax.broadcasted_iota(jnp.int32, columns, axis).reshape(head_count, -1)

    source = lax.rem(head_index - index_of(0) + head_count, head_count) * seq_count + seq_index
    slot = 2 * source + index_of(2)
    spans = jnp.arange(slot_count, dtype=jnp.int32)
    wanted = 2 * (
        lax.rem(head_index - jnp.arange(head_count, dtype=jnp.int32) + head_count, head_count)
        * seq_count
        + seq_index
    )
    place = [
        jnp.sum(jnp.where(span_slots[None, :] == (wanted + k)[:, None], spans[None, :], 0), axis=1)
        for k in range(2)
    ]
    span_at = jnp.where(index_of(2) == 0, place[0][:, None], place[1][:, None])
    position = (index_of(1) * slot_count + span_at) * span_rows + index_of(3)
    alive = (position < length).reshape(-1)
    column_kv = index_of(4).reshape(-1)
    kv_range = jnp.arange(kv_local, dtype=jnp.int32)
    bias = jnp.where(
        alive[None, :] & (column_kv[None, :] == kv_range[:, None]), 0.0, DEAD
    ).astype(F32)

    shape = (kv_local, token_count, group_size, token_count * kv_local)
    new_kv = lax.broadcasted_iota(jnp.int32, shape, 3) % kv_local
    new_depth = jnp.broadcast_to(decode_offsets[:, None], (token_count, kv_local)).reshape(-1)
    seen = (
        (new_depth[None, None, None, :] <= decode_offsets[None, :, None, None])
        & (new_kv == lax.broadcasted_iota(jnp.int32, shape, 0))
        & (seq_index == 0)
    )
    new_bias = jnp.where(seen, 0.0, DEAD).astype(F32)
    state = attend(
        queries,
        new_keys.reshape(token_count * kv_local, head_dim),
        new_values.reshape(token_count * kv_local, head_dim),
        new_bias.reshape(kv_local, token_count * group_size, token_count * kv_local),
        bias,
        blocks,
        score_scale,
    )
    stride = 1
    while stride < seq_count:
        last = 2 * stride >= seq_count
        other = lax.ppermute(state, "seq", [(s, s ^ stride) for s in range(seq_count)])
        state = merge(state, other, last)
        stride *= 2

    live = jnp.clip(length - shard_start, 0, shard_rows) * kv_local
    relaid_keys, relaid_values = relay(
        span_slots,
        live.reshape(1),
        got.reshape(cycle_size, 2, 2, span_rows * kv_local, head_dim),
    )
    whole = (shard_rows, kv_local, head_dim)
    return (
        relaid_keys.reshape(whole),
        relaid_values.reshape(whole),
        state.reshape(token_count, heads, head_dim),
    )


def solution(mesh):
    return jax.shard_map(
        step,
        mesh=mesh,
        in_specs=(
            P(("rep", "head", "seq"), None, None),
            P(("rep", "head", "seq"), None, None),
            P("rep"),
            P("rep"),
            P("rep", "head", None),
            P("rep", "head", None),
            P("rep", "head", None),
            P("rep"),
        ),
        out_specs=(
            P(("rep", "seq"), "head", None),
            P(("rep", "seq"), "head", None),
            P("rep", "head", None),
        ),
        check_vma=False,
    )
```

```python
import functools
import math

import jax
import jax.numpy as jnp
from jax import lax
from jax.experimental import pallas as pl
from jax.experimental.pallas import tpu as pltpu
from jax.sharding import PartitionSpec as P


BF16 = jnp.bfloat16
F32 = jnp.float32
DEAD = -1e30
STAT_ROWS = 16
LANES = 128
VMEM = pl.BlockSpec(memory_space=pltpu.VMEM)
SMEM = pl.BlockSpec(memory_space=pltpu.SMEM)
HBM = pl.BlockSpec(memory_space=pltpu.HBM)
PARAMS = pltpu.CompilerParams(vmem_limit_bytes=16 * 1024 * 1024)


def dot_rows(a, b):
    return lax.dot_general(a, b, (((1,), (1,)), ((), ())), preferred_element_type=F32)


def three_parts(x):
    high = x.astype(BF16).astype(F32)
    rest = x - high
    middle = rest.astype(BF16).astype(F32)
    return [high, middle, rest - middle]


def stacked(parts, like):
    row = lax.broadcasted_iota(jnp.int32, like, 0)
    out = jnp.zeros(like, F32)
    for at, part in enumerate(parts):
        out = jnp.where(row == at, part, out)
    return out.astype(BF16)


def eye(rows, columns):
    return (
        lax.broadcasted_iota(jnp.int32, (rows, columns), 0)
        == lax.broadcasted_iota(jnp.int32, (rows, columns), 1)
    ).astype(F32).astype(BF16)


def split_off(x, n):
    if n & (n - 1) == 0:
        return x & (n - 1), x >> (n.bit_length() - 1)
    return lax.rem(x, n), lax.div(x, n)


def pack_kernel(
    span_rows,
    group,
    keys_ref,
    values_ref,
    slots_hbm,
    length_hbm,
    depth_hbm,
    send_ref,
    mine_ref,
    away_ref,
    bias_ref,
    new_bias_ref,
    slots_ref,
    length_ref,
    depth_ref,
    in_sems,
    out_sems,
    fact_sems,
):
    seq_count, _, head_count, kv_count, _ = keys_ref.shape
    slot_count = slots_hbm.shape[0]
    token_count = depth_hbm.shape[0]
    me = lax.axis_index("head")
    seq_index = lax.axis_index("seq")
    facts = [
        pltpu.make_async_copy(source, target, fact_sems.at[at])
        for at, (source, target) in enumerate(
            ((slots_hbm, slots_ref), (length_hbm, length_ref), (depth_hbm, depth_ref))
        )
    ]
    blocks = []
    for shift in list(range(1, head_count)) + [0]:
        h = lax.rem(me + shift, head_count)
        for c, source in enumerate((keys_ref, values_ref)):
            target = away_ref.at[shift - 1, c] if shift else mine_ref.at[c]
            copy = pltpu.make_async_copy(source.at[:, :, h], target, in_sems.at[shift, c])
            copy.start()
            out = pltpu.make_async_copy(target, send_ref.at[h, :, c], out_sems.at[shift, c])
            blocks.append((copy, out))
    for fact in facts:
        fact.start()
    for fact in facts:
        fact.wait()

    wanted = []
    for b in range(head_count):
        first = 2 * (lax.rem(me + head_count - b, head_count) * seq_count + seq_index)
        wanted += [first, first + 1]

    def look(t, places):
        slot = slots_ref[t]
        return tuple(jnp.where(slot == w, t, p) for w, p in zip(wanted, places))

    places = lax.fori_loop(0, slot_count, look, tuple(jnp.int32(0) for _ in wanted))
    column = lax.broadcasted_iota(jnp.int32, (1, bias_ref.shape[1]), 1)
    kv, rest = split_off(column, kv_count)
    row, rest = split_off(rest, span_rows)
    half, rest = split_off(rest, 2)
    turn, block = split_off(rest, seq_count)
    span = jnp.zeros_like(column)
    for at, place in enumerate(places):
        span = jnp.where(2 * block + half == at, place, span)
    alive = (turn * slot_count + span) * span_rows + row < length_ref[0]
    for g in range(kv_count):
        bias_ref[g : g + 1, :] = jnp.where(alive & (kv == g), 0.0, DEAD)

    column = lax.broadcasted_iota(jnp.int32, (1, new_bias_ref.shape[2]), 1)
    kv, token = split_off(column, kv_count)
    depth = jnp.zeros_like(column)
    for t in range(token_count):
        depth = jnp.where(token == t, depth_ref[t], depth)
    for t in range(token_count):
        limit = jnp.where(seq_index == 0, depth_ref[t], -1)
        for g in range(kv_count):
            seen = jnp.where((depth <= limit) & (kv == g), 0.0, DEAD)
            new_bias_ref[g, t * group : (t + 1) * group, :] = jnp.broadcast_to(
                seen, (group, seen.shape[1])
            )

    for copy, out in blocks:
        copy.wait()
        out.start()
    for _, out in blocks:
        out.wait()


def pack(cache_keys, cache_values, span_slots, prompt_length, depth, seq_count, head_count, heads):
    row_count, kv_all, head_dim = cache_keys.shape
    kv = kv_all // head_count
    rows = row_count // seq_count
    split = (seq_count, rows, head_count, kv, head_dim)
    block = (seq_count, rows, kv, head_dim)
    tokens = depth.shape[0]
    group = heads // kv
    inputs = [
        pltpu.with_memory_space_constraint(x.reshape(split), pltpu.HBM)
        for x in (cache_keys, cache_values)
    ]
    return pl.pallas_call(
        functools.partial(pack_kernel, rows // 2, group),
        out_shape=(
            jax.ShapeDtypeStruct((head_count, seq_count, 2, rows, kv, head_dim), BF16),
            jax.ShapeDtypeStruct((2,) + block, BF16),
            jax.ShapeDtypeStruct((head_count - 1, 2) + block, BF16),
            jax.ShapeDtypeStruct((kv, head_count * row_count * kv), F32),
            jax.ShapeDtypeStruct((kv, tokens * group, tokens * kv), F32),
        ),
        in_specs=[HBM] * 5,
        out_specs=(HBM, VMEM, VMEM, VMEM, VMEM),
        scratch_shapes=[
            pltpu.SMEM(span_slots.shape, jnp.int32),
            pltpu.SMEM(prompt_length.shape, jnp.int32),
            pltpu.SMEM(depth.shape, jnp.int32),
            pltpu.SemaphoreType.DMA((head_count, 2)),
            pltpu.SemaphoreType.DMA((head_count, 2)),
            pltpu.SemaphoreType.DMA((3,)),
        ],
        compiler_params=PARAMS,
        name="pack",
    )(*inputs, span_slots, prompt_length, depth)


def attend_kernel(score_scale, query_ref, new_keys_ref, new_values_ref, new_bias_ref, bias_ref, *rest):
    *block_refs, out_ref, rows_buf, stat_buf = rest
    tokens, heads, head_dim = query_ref.shape
    kv_count = bias_ref.shape[0]
    group = heads // kv_count
    lane = lax.broadcasted_iota(jnp.int32, (tokens * group, head_dim), 1)
    keys = jnp.concatenate([ref[0] for ref in block_refs], axis=0)
    values = jnp.concatenate([ref[1] for ref in block_refs], axis=0)
    for g in range(kv_count):
        query = query_ref[:, g * group : (g + 1) * group, :].reshape(tokens * group, head_dim)
        scores = dot_rows(query, keys) * score_scale + bias_ref[g : g + 1, :]
        fresh = dot_rows(query, new_keys_ref[...]) * score_scale + new_bias_ref[g]
        peak = jnp.maximum(
            jnp.max(scores, axis=1, keepdims=True), jnp.max(fresh, axis=1, keepdims=True)
        )
        weights = jnp.exp(scores - peak)
        fresh = jnp.exp(fresh - peak)
        total = jnp.sum(weights, axis=1, keepdims=True) + jnp.sum(fresh, axis=1, keepdims=True)
        weighted = jnp.dot(weights.astype(BF16), values, preferred_element_type=F32)
        weighted = weighted + jnp.dot(
            fresh.astype(BF16), new_values_ref[...], preferred_element_type=F32
        )
        stats = jnp.zeros((tokens * group, head_dim), F32)
        for at, part in enumerate(three_parts(peak) + three_parts(total)):
            stats = jnp.where(lane == at, part, stats)
        rows_buf[:, g] = weighted.astype(BF16).reshape(tokens, group, head_dim)
        stat_buf[:, g] = stats.astype(BF16).reshape(tokens, group, head_dim)
    count = tokens * heads
    out_ref[:count, :] = rows_buf[...].reshape(count, head_dim)
    turned = dot_rows(eye(STAT_ROWS, head_dim), stat_buf[...].reshape(count, head_dim))
    for at in range(count // LANES):
        start = count + at * STAT_ROWS
        out_ref[start : start + STAT_ROWS, :] = turned[:, at * LANES : (at + 1) * LANES].astype(BF16)


def attend(query, new_keys, new_values, new_bias, bias, blocks, score_scale):
    tokens, heads, head_dim = query.shape
    kv_count = bias.shape[0]
    group = heads // kv_count
    count = tokens * heads
    return pl.pallas_call(
        functools.partial(attend_kernel, score_scale),
        out_shape=jax.ShapeDtypeStruct((count + count // LANES * STAT_ROWS, head_dim), BF16),
        in_specs=[VMEM] * (5 + len(blocks)),
        out_specs=VMEM,
        scratch_shapes=[
            pltpu.VMEM((tokens, kv_count, group, head_dim), BF16),
            pltpu.VMEM((tokens, kv_count, group, head_dim), BF16),
        ],
        compiler_params=PARAMS,
        name="attend",
    )(query, new_keys, new_values, new_bias, bias, *blocks)


def tree(combine, parts):
    while len(parts) > 1:
        parts = [combine(parts[k], parts[k + 1]) for k in range(0, len(parts), 2)]
    return parts[0]


def merge_kernel(last, *refs):
    *in_refs, out_ref = refs
    head_dim = out_ref.shape[1]
    count = in_refs[0].shape[0] * LANES // (LANES + STAT_ROWS)
    turn = eye(LANES, LANES)
    factor_rows = -(-3 * len(in_refs) // STAT_ROWS) * STAT_ROWS
    for at in range(count // LANES):
        start = count + at * STAT_ROWS
        peaks, totals = [], []
        for ref in in_refs:
            stats = ref[start : start + STAT_ROWS, :].astype(F32)
            peaks.append(stats[0:1] + stats[1:2] + stats[2:3])
            totals.append(stats[3:4] + stats[4:5] + stats[5:6])
        peak = tree(jnp.maximum, peaks)
        factors = [jnp.exp(p - peak) for p in peaks]
        total = tree(jnp.add, [f * t for f, t in zip(factors, totals)])
        if last:
            factors = [f / total for f in factors]
        else:
            out_ref[start : start + STAT_ROWS, :] = stacked(
                three_parts(peak) + three_parts(total), (STAT_ROWS, LANES)
            )
        parts = [part for f in factors for part in three_parts(f)]
        columns = dot_rows(turn, stacked(parts, (factor_rows, LANES)))
        terms = []
        for k, ref in enumerate(in_refs):
            column = columns[:, 3 * k : 3 * k + 1] + columns[:, 3 * k + 1 : 3 * k + 2]
            column = jnp.broadcast_to(column + columns[:, 3 * k + 2 : 3 * k + 3], (LANES, head_dim))
            terms.append(ref[at * LANES : (at + 1) * LANES, :].astype(F32) * column)
        out_ref[at * LANES : (at + 1) * LANES, :] = tree(jnp.add, terms).astype(BF16)


def merge(states, last):
    rows, head_dim = states[0].shape
    if last:
        rows = rows * LANES // (LANES + STAT_ROWS)
    return pl.pallas_call(
        functools.partial(merge_kernel, last),
        out_shape=jax.ShapeDtypeStruct((rows, head_dim), BF16),
        in_specs=[VMEM] * len(states),
        out_specs=VMEM,
        compiler_params=PARAMS,
        name="merge",
    )(*states)


def relay_kernel(slots_ref, live_ref, got_ref, keys_ref, values_ref):
    slot_count, span, head_dim = keys_ref.shape
    row = lax.broadcasted_iota(jnp.int32, (span, head_dim), 0)
    live = live_ref[0]

    def one(t, carry):
        slot = slots_ref[t]
        kept = row < live - t * span
        for c, out_ref in enumerate((keys_ref, values_ref)):
            block = got_ref[slot // 2, c, slot % 2].astype(F32)
            out_ref[t] = jnp.where(kept, block, 0.0).astype(BF16)
        return carry

    lax.fori_loop(0, slot_count, one, 0, unroll=4)


def relay(span_slots, live, got):
    _, _, _, span, head_dim = got.shape
    shape = jax.ShapeDtypeStruct((span_slots.shape[0], span, head_dim), BF16)
    return pl.pallas_call(
        relay_kernel,
        out_shape=(shape, shape),
        in_specs=[SMEM, SMEM, VMEM],
        out_specs=(VMEM, VMEM),
        compiler_params=PARAMS,
        name="relay",
    )(span_slots, live, got)


def step(
    cache_keys,
    cache_values,
    span_slots,
    prompt_length,
    queries,
    new_keys,
    new_values,
    decode_offsets,
):
    row_count, kv_all, head_dim = cache_keys.shape
    seq_count = lax.axis_size("seq")
    head_count = lax.axis_size("head")
    cycle_size = seq_count * head_count
    slot_count = span_slots.shape[0]
    span_rows = row_count // (2 * seq_count)
    kv_local = kv_all // head_count
    token_count, heads, _ = queries.shape
    length = prompt_length[0]
    score_scale = 1.0 / math.sqrt(head_dim)
    shard_rows = slot_count * span_rows
    seq_index = lax.axis_index("seq")
    shard_start = seq_index * shard_rows

    packed, mine, away, bias, new_bias = pack(
        cache_keys,
        cache_values,
        span_slots,
        prompt_length,
        decode_offsets,
        seq_count,
        head_count,
        heads,
    )
    flat = (2, row_count * kv_local, head_dim)
    blocks = [mine.reshape(flat)]
    for shift in range(1, head_count):
        blocks.append(
            lax.ppermute(
                away[shift - 1].reshape(flat),
                "head",
                [(h, (h + shift) % head_count) for h in range(head_count)],
            )
        )
    got = lax.all_to_all(
        packed.reshape(cycle_size, 2, 2 * span_rows * kv_local, head_dim),
        ("head", "seq"),
        split_axis=0,
        concat_axis=0,
        tiled=True,
    )

    state = attend(
        queries,
        new_keys.reshape(token_count * kv_local, head_dim),
        new_values.reshape(token_count * kv_local, head_dim),
        new_bias,
        bias,
        blocks,
        score_scale,
    )
    stride = 1
    while stride < seq_count:
        ways = 4 if stride == 1 and seq_count > 4 else 2
        last = stride * ways >= seq_count
        states = [state]
        for way in range(1, ways):
            pairs = [(s, s ^ (way * stride)) for s in range(seq_count)]
            states.append(lax.ppermute(state, "seq", pairs))
        state = merge(states, last)
        stride *= ways

    live = jnp.clip(length - shard_start, 0, shard_rows) * kv_local
    relaid_keys, relaid_values = relay(
        span_slots,
        live.reshape(1),
        got.reshape(cycle_size, 2, 2, span_rows * kv_local, head_dim),
    )
    whole = (shard_rows, kv_local, head_dim)
    return (
        relaid_keys.reshape(whole),
        relaid_values.reshape(whole),
        state.reshape(token_count, heads, head_dim),
    )


def solution(mesh):
    return jax.shard_map(
        step,
        mesh=mesh,
        in_specs=(
            P(("rep", "head", "seq"), None, None),
            P(("rep", "head", "seq"), None, None),
            P("rep"),
            P("rep"),
            P("rep", "head", None),
            P("rep", "head", None),
            P("rep", "head", None),
            P("rep"),
        ),
        out_specs=(
            P(("rep", "seq"), "head", None),
            P(("rep", "seq"), "head", None),
            P("rep", "head", None),
        ),
        check_vma=False,
    )
```

```python
import functools
import math

import jax
import jax.numpy as jnp
from jax import lax
from jax.experimental import pallas as pl
from jax.experimental.pallas import tpu as pltpu
from jax.sharding import PartitionSpec as P


BF16 = jnp.bfloat16
F32 = jnp.float32
DEAD = -1e30
STAT_ROWS = 16
WIDE_ROWS = 8
LANES = 128
VMEM = pl.BlockSpec(memory_space=pltpu.VMEM)
SMEM = pl.BlockSpec(memory_space=pltpu.SMEM)
HBM = pl.BlockSpec(memory_space=pltpu.HBM)
PARAMS = pltpu.CompilerParams(vmem_limit_bytes=16 * 1024 * 1024)


def dot_rows(a, b):
    return lax.dot_general(a, b, (((1,), (1,)), ((), ())), preferred_element_type=F32)


def three_parts(x):
    high = x.astype(BF16).astype(F32)
    rest = x - high
    middle = rest.astype(BF16).astype(F32)
    return [high, middle, rest - middle]


def stacked(parts, like):
    row = lax.broadcasted_iota(jnp.int32, like, 0)
    out = jnp.zeros(like, F32)
    for at, part in enumerate(parts):
        out = jnp.where(row == at, part, out)
    return out.astype(BF16)


def eye(rows, columns):
    return (
        lax.broadcasted_iota(jnp.int32, (rows, columns), 0)
        == lax.broadcasted_iota(jnp.int32, (rows, columns), 1)
    ).astype(F32).astype(BF16)


def split_off(x, n):
    if n & (n - 1) == 0:
        return x & (n - 1), x >> (n.bit_length() - 1)
    return lax.rem(x, n), lax.div(x, n)


def pack_kernel(
    span_rows,
    group,
    keys_ref,
    values_ref,
    slots_hbm,
    length_ref,
    depth_hbm,
    *rest,
):
    staged, (send_ref, mine_ref, away_ref, bias_ref, new_bias_ref) = rest[:3], rest[3:8]
    targets = rest[8:11]
    slots_ref, depth_ref, in_sems, out_sems, fact_sems, stage_sems = rest[11:]
    seq_count, _, head_count, kv_count, _ = keys_ref.shape
    slot_count = slots_hbm.shape[0]
    token_count = depth_hbm.shape[0]
    me = lax.axis_index("head")
    seq_index = lax.axis_index("seq")
    facts = [
        pltpu.make_async_copy(source, target, fact_sems.at[at])
        for at, (source, target) in enumerate(
            ((slots_hbm, slots_ref), (depth_hbm, depth_ref))
        )
    ]
    blocks = []
    for shift in list(range(1, head_count)) + [0]:
        h = lax.rem(me + shift, head_count)
        for c, source in enumerate((keys_ref, values_ref)):
            target = away_ref.at[shift - 1, c] if shift else mine_ref.at[c]
            copy = pltpu.make_async_copy(source.at[:, :, h], target, in_sems.at[shift, c])
            copy.start()
            out = pltpu.make_async_copy(target, send_ref.at[h, :, c], out_sems.at[shift, c])
            blocks.append((copy, out))
    stages = [
        pltpu.make_async_copy(source, target, stage_sems.at[at])
        for at, (source, target) in enumerate(zip(staged, targets))
    ]
    for copy in facts + stages:
        copy.start()
    for fact in facts:
        fact.wait()

    wanted = []
    for b in range(head_count):
        first = 2 * (lax.rem(me + head_count - b, head_count) * seq_count + seq_index)
        wanted += [first, first + 1]

    def look(t, places):
        slot = slots_ref[t]
        return tuple(jnp.where(slot == w, t, p) for w, p in zip(wanted, places))

    places = lax.fori_loop(0, slot_count, look, tuple(jnp.int32(0) for _ in wanted))
    column = lax.broadcasted_iota(jnp.int32, (1, bias_ref.shape[1]), 1)
    kv, rest = split_off(column, kv_count)
    row, rest = split_off(rest, span_rows)
    half, rest = split_off(rest, 2)
    turn, block = split_off(rest, seq_count)
    span = jnp.zeros_like(column)
    for at, place in enumerate(places):
        span = jnp.where(2 * block + half == at, place, span)
    alive = (turn * slot_count + span) * span_rows + row < length_ref[0]
    for g in range(kv_count):
        bias_ref[g : g + 1, :] = jnp.where(alive & (kv == g), 0.0, DEAD)

    column = lax.broadcasted_iota(jnp.int32, (1, new_bias_ref.shape[2]), 1)
    kv, token = split_off(column, kv_count)
    depth = jnp.zeros_like(column)
    for t in range(token_count):
        depth = jnp.where(token == t, depth_ref[t], depth)
    for t in range(token_count):
        limit = jnp.where(seq_index == 0, depth_ref[t], -1)
        for g in range(kv_count):
            seen = jnp.where((depth <= limit) & (kv == g), 0.0, DEAD)
            new_bias_ref[g, t * group : (t + 1) * group, :] = jnp.broadcast_to(
                seen, (group, seen.shape[1])
            )

    for copy, out in blocks:
        copy.wait()
        out.start()
    for _, out in blocks:
        out.wait()
    for copy in stages:
        copy.wait()


def pack(
    cache_keys,
    cache_values,
    span_slots,
    prompt_length,
    depth,
    queries,
    new_keys,
    new_values,
    seq_count,
    head_count,
):
    row_count, kv_all, head_dim = cache_keys.shape
    kv = kv_all // head_count
    rows = row_count // seq_count
    split = (seq_count, rows, head_count, kv, head_dim)
    block = (seq_count, rows, kv, head_dim)
    tokens, heads, _ = queries.shape
    group = heads // kv
    fresh = (tokens * kv, head_dim)
    inputs = [
        x if x is prompt_length else pltpu.with_memory_space_constraint(x, pltpu.HBM)
        for x in (
            cache_keys.reshape(split),
            cache_values.reshape(split),
            span_slots,
            prompt_length,
            depth,
            queries,
            new_keys.reshape(fresh),
            new_values.reshape(fresh),
        )
    ]
    return pl.pallas_call(
        functools.partial(pack_kernel, rows // 2, group),
        out_shape=(
            jax.ShapeDtypeStruct((head_count, seq_count, 2, rows, kv, head_dim), BF16),
            jax.ShapeDtypeStruct((2,) + block, BF16),
            jax.ShapeDtypeStruct((head_count - 1, 2) + block, BF16),
            jax.ShapeDtypeStruct((kv, head_count * row_count * kv), F32),
            jax.ShapeDtypeStruct((kv, tokens * group, tokens * kv), F32),
            jax.ShapeDtypeStruct(queries.shape, BF16),
            jax.ShapeDtypeStruct(fresh, BF16),
            jax.ShapeDtypeStruct(fresh, BF16),
        ),
        in_specs=[HBM] * 3 + [SMEM] + [HBM] * 4,
        out_specs=(HBM,) + (VMEM,) * 7,
        scratch_shapes=[
            pltpu.SMEM(span_slots.shape, jnp.int32),
            pltpu.SMEM(depth.shape, jnp.int32),
            pltpu.SemaphoreType.DMA((head_count, 2)),
            pltpu.SemaphoreType.DMA((head_count, 2)),
            pltpu.SemaphoreType.DMA((2,)),
            pltpu.SemaphoreType.DMA((3,)),
        ],
        compiler_params=PARAMS,
        name="pack",
    )(*inputs)


def attend_kernel(
    score_scale, ways, query_ref, new_keys_ref, new_values_ref, new_bias_ref, bias_ref, *rest
):
    *block_refs, rows_buf, stat_buf = rest
    block_refs, out_refs = block_refs[:-ways], block_refs[-ways:]
    tokens, heads, head_dim = query_ref.shape
    kv_count = bias_ref.shape[0]
    group = heads // kv_count
    lane = lax.broadcasted_iota(jnp.int32, (tokens * group, head_dim), 1)
    keys = jnp.concatenate([ref[0] for ref in block_refs], axis=0)
    values = jnp.concatenate([ref[1] for ref in block_refs], axis=0)
    for g in range(kv_count):
        query = query_ref[:, g * group : (g + 1) * group, :].reshape(tokens * group, head_dim)
        scores = dot_rows(query, keys) * score_scale + bias_ref[g : g + 1, :]
        fresh = dot_rows(query, new_keys_ref[...]) * score_scale + new_bias_ref[g]
        peak = jnp.maximum(
            jnp.max(scores, axis=1, keepdims=True), jnp.max(fresh, axis=1, keepdims=True)
        )
        weights = jnp.exp(scores - peak)
        fresh = jnp.exp(fresh - peak)
        total = jnp.sum(weights, axis=1, keepdims=True) + jnp.sum(fresh, axis=1, keepdims=True)
        weighted = jnp.dot(weights.astype(BF16), values, preferred_element_type=F32)
        weighted = weighted + jnp.dot(
            fresh.astype(BF16), new_values_ref[...], preferred_element_type=F32
        )
        stats = jnp.zeros((tokens * group, head_dim), F32)
        for at, part in enumerate(three_parts(peak) + three_parts(total)):
            stats = jnp.where(lane == at, part, stats)
        rows_buf[:, g] = weighted.astype(BF16).reshape(tokens, group, head_dim)
        stat_buf[:, g] = stats.astype(BF16).reshape(tokens, group, head_dim)
    here = lax.rem(lax.axis_index("seq"), ways)
    share = tokens // ways
    per = share * heads
    pick = eye(STAT_ROWS, head_dim)
    for way, out_ref in enumerate(out_refs):
        first = lax.bitwise_xor(here, way) * share
        out_ref[:per, :] = rows_buf[pl.ds(first, share)].reshape(per, head_dim)
        turned = dot_rows(pick, stat_buf[pl.ds(first, share)].reshape(per, head_dim)).astype(BF16)
        for at in range(per // LANES):
            start = per + at * STAT_ROWS
            out_ref[start : start + STAT_ROWS, :] = turned[:, at * LANES : (at + 1) * LANES]


def attend(query, new_keys, new_values, new_bias, bias, blocks, score_scale, ways):
    tokens, heads, head_dim = query.shape
    kv_count = bias.shape[0]
    group = heads // kv_count
    per = tokens * heads // ways
    piece = jax.ShapeDtypeStruct((per + per // LANES * STAT_ROWS, head_dim), BF16)
    return pl.pallas_call(
        functools.partial(attend_kernel, score_scale, ways),
        out_shape=(piece,) * ways,
        in_specs=[VMEM] * (5 + len(blocks)),
        out_specs=(VMEM,) * ways,
        scratch_shapes=[
            pltpu.VMEM((tokens, kv_count, group, head_dim), BF16),
            pltpu.VMEM((tokens, kv_count, group, head_dim), BF16),
        ],
        compiler_params=PARAMS,
        name="attend",
    )(query, new_keys, new_values, new_bias, bias, *blocks)


def tree(combine, parts):
    while len(parts) > 1:
        parts = [combine(parts[k], parts[k + 1]) for k in range(0, len(parts), 2)]
    return parts[0]


def merge_kernel(per, last, *refs):
    *in_refs, out_ref = refs
    head_dim = out_ref.shape[1]
    chunks = per // LANES
    rows_in = (in_refs[0].shape[0] - per) // chunks
    split = in_refs[0].dtype == BF16
    turn = eye(LANES, LANES)
    factor_rows = -(-3 * len(in_refs) // STAT_ROWS) * STAT_ROWS
    for at in range(chunks):
        peaks, totals = [], []
        for ref in in_refs:
            stats = ref[per + at * rows_in : per + (at + 1) * rows_in, :].astype(F32)
            if split:
                peaks.append(stats[0:1] + stats[1:2] + stats[2:3])
                totals.append(stats[3:4] + stats[4:5] + stats[5:6])
            else:
                peaks.append(stats[0:1])
                totals.append(stats[1:2])
        peak = tree(jnp.maximum, peaks)
        factors = [jnp.exp(p - peak) for p in peaks]
        total = tree(jnp.add, [f * t for f, t in zip(factors, totals)])
        if last:
            factors = [f / total for f in factors]
        else:
            start = per + at * WIDE_ROWS
            row = lax.broadcasted_iota(jnp.int32, (WIDE_ROWS, LANES), 0)
            out_ref[start : start + WIDE_ROWS, :] = jnp.where(row == 0, peak, total)
        parts = [part for f in factors for part in three_parts(f)]
        columns = dot_rows(turn, stacked(parts, (factor_rows, LANES)))
        terms = []
        for k, ref in enumerate(in_refs):
            column = columns[:, 3 * k : 3 * k + 1] + columns[:, 3 * k + 1 : 3 * k + 2]
            column = jnp.broadcast_to(column + columns[:, 3 * k + 2 : 3 * k + 3], (LANES, head_dim))
            terms.append(ref[at * LANES : (at + 1) * LANES, :].astype(F32) * column)
        out_ref[at * LANES : (at + 1) * LANES, :] = tree(jnp.add, terms).astype(out_ref.dtype)


def merge(states, per, last):
    head_dim = states[0].shape[1]
    if last:
        out = jax.ShapeDtypeStruct((per, head_dim), BF16)
    else:
        out = jax.ShapeDtypeStruct((per + per // LANES * WIDE_ROWS, head_dim), F32)
    return pl.pallas_call(
        functools.partial(merge_kernel, per, last),
        out_shape=out,
        in_specs=[VMEM] * len(states),
        out_specs=VMEM,
        compiler_params=PARAMS,
        name="merge",
    )(*states)


def join_kernel(*refs):
    *in_refs, out_ref, sems = refs
    ways = len(in_refs)
    per = in_refs[0].shape[0]
    here = lax.rem(lax.axis_index("seq"), ways)
    copies = []
    for way, ref in enumerate(in_refs):
        start = pl.multiple_of(lax.bitwise_xor(here, way) * per, per)
        copies.append(pltpu.make_async_copy(ref, out_ref.at[pl.ds(start, per)], sems.at[way]))
        copies[-1].start()
    for copy in copies:
        copy.wait()


def join(pieces):
    per, head_dim = pieces[0].shape
    return pl.pallas_call(
        join_kernel,
        out_shape=jax.ShapeDtypeStruct((len(pieces) * per, head_dim), BF16),
        in_specs=[VMEM] * len(pieces),
        out_specs=HBM,
        scratch_shapes=[pltpu.SemaphoreType.DMA((len(pieces),))],
        compiler_params=PARAMS,
        name="join",
    )(*pieces)


def relay_kernel(kv_count, slots_hbm, length_ref, got_ref, keys_ref, values_ref, slots_ref, sem):
    copy = pltpu.make_async_copy(slots_hbm, slots_ref, sem)
    copy.start()
    copy.wait()
    slot_count, span, head_dim = keys_ref.shape
    row = lax.broadcasted_iota(jnp.int32, (span, head_dim), 0)
    live = length_ref[0] * kv_count - lax.axis_index("seq") * (slot_count * span)

    def one(t, carry):
        slot = slots_ref[t]
        kept = row < live - t * span
        for c, out_ref in enumerate((keys_ref, values_ref)):
            block = got_ref[slot // 2, c, slot % 2].astype(F32)
            out_ref[t] = jnp.where(kept, block, 0.0).astype(BF16)
        return carry

    lax.fori_loop(0, slot_count, one, 0, unroll=4)


def relay(span_slots, prompt_length, got, kv_count):
    _, _, _, span, head_dim = got.shape
    shape = jax.ShapeDtypeStruct((span_slots.shape[0], span, head_dim), BF16)
    return pl.pallas_call(
        functools.partial(relay_kernel, kv_count),
        out_shape=(shape, shape),
        in_specs=[HBM, SMEM, VMEM],
        out_specs=(VMEM, VMEM),
        scratch_shapes=[pltpu.SMEM(span_slots.shape, jnp.int32), pltpu.SemaphoreType.DMA],
        compiler_params=PARAMS,
        name="relay",
    )(pltpu.with_memory_space_constraint(span_slots, pltpu.HBM), prompt_length, got)


def step(
    cache_keys,
    cache_values,
    span_slots,
    prompt_length,
    queries,
    new_keys,
    new_values,
    decode_offsets,
):
    row_count, kv_all, head_dim = cache_keys.shape
    seq_count = lax.axis_size("seq")
    head_count = lax.axis_size("head")
    cycle_size = seq_count * head_count
    slot_count = span_slots.shape[0]
    span_rows = row_count // (2 * seq_count)
    kv_local = kv_all // head_count
    token_count, heads, _ = queries.shape
    score_scale = 1.0 / math.sqrt(head_dim)
    shard_rows = slot_count * span_rows
    ways = math.gcd(4, seq_count)

    packed, mine, away, bias, new_bias, query, fresh_keys, fresh_values = pack(
        cache_keys,
        cache_values,
        span_slots,
        prompt_length,
        decode_offsets,
        queries,
        new_keys,
        new_values,
        seq_count,
        head_count,
    )
    flat = (2, row_count * kv_local, head_dim)
    blocks = [mine.reshape(flat)]
    for shift in range(1, head_count):
        blocks.append(
            lax.ppermute(
                away[shift - 1].reshape(flat),
                "head",
                [(h, (h + shift) % head_count) for h in range(head_count)],
            )
        )
    got = lax.all_to_all(
        packed.reshape(cycle_size, 2, 2 * span_rows * kv_local, head_dim),
        ("head", "seq"),
        split_axis=0,
        concat_axis=0,
        tiled=True,
    )

    pieces = attend(
        query, fresh_keys, fresh_values, new_bias, bias, blocks, score_scale, ways
    )
    per = token_count * heads // ways

    def swapped(x, distance):
        return lax.ppermute(x, "seq", [(s, s ^ distance) for s in range(seq_count)])

    states = [pieces[0]] + [swapped(pieces[way], way) for way in range(1, ways)]
    distance = ways
    state = merge(states, per, distance >= seq_count)
    while distance < seq_count:
        other = swapped(state, distance)
        distance *= 2
        state = merge([state, other], per, distance >= seq_count)
    finished = [state] + [swapped(state, way) for way in range(1, ways)]
    attended = join(finished)

    relaid_keys, relaid_values = relay(
        span_slots,
        prompt_length,
        got.reshape(cycle_size, 2, 2, span_rows * kv_local, head_dim),
        kv_local,
    )
    whole = (shard_rows, kv_local, head_dim)
    return (
        relaid_keys.reshape(whole),
        relaid_values.reshape(whole),
        attended.reshape(token_count, heads, head_dim),
    )


def solution(mesh):
    return jax.shard_map(
        step,
        mesh=mesh,
        in_specs=(
            P(("rep", "head", "seq"), None, None),
            P(("rep", "head", "seq"), None, None),
            P("rep"),
            P("rep"),
            P("rep", "head", None),
            P("rep", "head", None),
            P("rep", "head", None),
            P("rep"),
        ),
        out_specs=(
            P(("rep", "seq"), "head", None),
            P(("rep", "seq"), "head", None),
            P("rep", "head", None),
        ),
        check_vma=False,
    )
```

```python
import functools
import math

import jax
import jax.numpy as jnp
from jax import lax
from jax.experimental import pallas as pl
from jax.experimental.pallas import tpu as pltpu
from jax.sharding import PartitionSpec as P


BF16 = jnp.bfloat16
F32 = jnp.float32
DEAD = -1e30
NOWHERE = 1 << 30
STAT_ROWS = 16
WIDE_ROWS = 8
LANES = 128
VMEM = pl.BlockSpec(memory_space=pltpu.VMEM)
SMEM = pl.BlockSpec(memory_space=pltpu.SMEM)
HBM = pl.BlockSpec(memory_space=pltpu.HBM)
PARAMS = pltpu.CompilerParams(vmem_limit_bytes=16 * 1024 * 1024)


def dot_rows(a, b):
    return lax.dot_general(a, b, (((1,), (1,)), ((), ())), preferred_element_type=F32)


def three_parts(x):
    high = x.astype(BF16).astype(F32)
    rest = x - high
    middle = rest.astype(BF16).astype(F32)
    return [high, middle, rest - middle]


def stacked(parts, like):
    row = lax.broadcasted_iota(jnp.int32, like, 0)
    out = jnp.zeros(like, F32)
    for at, part in enumerate(parts):
        out = jnp.where(row == at, part, out)
    return out.astype(BF16)


def eye(rows, columns):
    return (
        lax.broadcasted_iota(jnp.int32, (rows, columns), 0)
        == lax.broadcasted_iota(jnp.int32, (rows, columns), 1)
    ).astype(F32).astype(BF16)


def split_off(x, n):
    if n & (n - 1) == 0:
        return x & (n - 1), x >> (n.bit_length() - 1)
    return lax.rem(x, n), lax.div(x, n)


def pack_kernel(
    span_rows,
    keys_ref,
    values_ref,
    slots_hbm,
    query_hbm,
    send_ref,
    mine_ref,
    away_ref,
    place_ref,
    query_ref,
    slots_ref,
    in_sems,
    out_sems,
    sems,
):
    seq_count, _, head_count, kv_count, _ = keys_ref.shape
    slot_count = slots_hbm.shape[0]
    me = lax.axis_index("head")
    seq_index = lax.axis_index("seq")
    facts = pltpu.make_async_copy(slots_hbm, slots_ref, sems.at[0])
    facts.start()
    staged = pltpu.make_async_copy(query_hbm, query_ref, sems.at[1])
    blocks = []
    for shift in list(range(1, head_count)) + [0]:
        h = lax.rem(me + shift, head_count)
        for c, source in enumerate((keys_ref, values_ref)):
            target = away_ref.at[shift - 1, c] if shift else mine_ref.at[c]
            copy = pltpu.make_async_copy(source.at[:, :, h], target, in_sems.at[shift, c])
            copy.start()
            out = pltpu.make_async_copy(target, send_ref.at[h, :, c], out_sems.at[shift, c])
            blocks.append((copy, out))
    staged.start()
    for copy, out in blocks:
        copy.wait()
        out.start()
    facts.wait()

    wanted = []
    for b in range(head_count):
        first = 2 * (lax.rem(me + head_count - b, head_count) * seq_count + seq_index)
        wanted += [first, first + 1]

    def look(t, places):
        slot = slots_ref[t]
        return tuple(jnp.where(slot == w, t, p) for w, p in zip(wanted, places))

    places = lax.fori_loop(0, slot_count, look, tuple(jnp.int32(0) for _ in wanted))
    column = lax.broadcasted_iota(jnp.int32, (1, place_ref.shape[1]), 1)
    kv, rest = split_off(column, kv_count)
    row, rest = split_off(rest, span_rows)
    half, rest = split_off(rest, 2)
    turn, block = split_off(rest, seq_count)
    span = jnp.zeros_like(column)
    for at, place in enumerate(places):
        span = jnp.where(2 * block + half == at, place, span)
    position = (turn * slot_count + span) * span_rows + row
    for g in range(kv_count):
        place_ref[g : g + 1, :] = jnp.where(kv == g, position, NOWHERE)
    for _, out in blocks:
        out.wait()
    staged.wait()


def pack(cache_keys, cache_values, span_slots, queries, seq_count, head_count):
    row_count, kv_all, head_dim = cache_keys.shape
    kv = kv_all // head_count
    rows = row_count // seq_count
    split = (seq_count, rows, head_count, kv, head_dim)
    block = (seq_count, rows, kv, head_dim)
    inputs = [
        pltpu.with_memory_space_constraint(x, pltpu.HBM)
        for x in (cache_keys.reshape(split), cache_values.reshape(split), span_slots, queries)
    ]
    return pl.pallas_call(
        functools.partial(pack_kernel, rows // 2),
        out_shape=(
            jax.ShapeDtypeStruct((head_count, seq_count, 2, rows, kv, head_dim), BF16),
            jax.ShapeDtypeStruct((2,) + block, BF16),
            jax.ShapeDtypeStruct((head_count - 1, 2) + block, BF16),
            jax.ShapeDtypeStruct((kv, head_count * row_count * kv), jnp.int32),
            jax.ShapeDtypeStruct(queries.shape, BF16),
        ),
        in_specs=[HBM] * len(inputs),
        out_specs=(HBM,) + (VMEM,) * 4,
        scratch_shapes=[
            pltpu.SMEM(span_slots.shape, jnp.int32),
            pltpu.SemaphoreType.DMA((head_count, 2)),
            pltpu.SemaphoreType.DMA((head_count, 2)),
            pltpu.SemaphoreType.DMA((2,)),
        ],
        compiler_params=PARAMS,
        name="pack",
    )(*inputs)


def softmax_parts(scores, values):
    peak = jnp.max(scores, axis=1, keepdims=True)
    weights = jnp.exp(scores - peak)
    total = jnp.sum(weights, axis=1, keepdims=True)
    weighted = jnp.dot(weights.astype(BF16), values, preferred_element_type=F32)
    return peak, total, weighted


def stat_lanes(peak, total, head_dim):
    lane = lax.broadcasted_iota(jnp.int32, (peak.shape[0], head_dim), 1)
    stats = jnp.zeros((peak.shape[0], head_dim), F32)
    for at, part in enumerate(three_parts(peak) + three_parts(total)):
        stats = jnp.where(lane == at, part, stats)
    return stats.astype(BF16)


def attend_kernel(score_scale, ways, length_ref, query_ref, place_ref, *rest):
    *block_refs, rows_buf, stat_buf = rest
    block_refs, out_refs = block_refs[:-ways], block_refs[-ways:]
    tokens, heads, head_dim = query_ref.shape
    kv_count = place_ref.shape[0]
    group = heads // kv_count
    keys = jnp.concatenate([ref[0] for ref in block_refs], axis=0)
    values = jnp.concatenate([ref[1] for ref in block_refs], axis=0)
    for g in range(kv_count):
        query = query_ref[:, g * group : (g + 1) * group, :].reshape(tokens * group, head_dim)
        bias = jnp.where(place_ref[g : g + 1, :] < length_ref[0], 0.0, DEAD)
        peak, total, weighted = softmax_parts(dot_rows(query, keys) * score_scale + bias, values)
        rows_buf[:, g] = weighted.astype(BF16).reshape(tokens, group, head_dim)
        stat_buf[:, g] = stat_lanes(peak, total, head_dim).reshape(tokens, group, head_dim)
    here = lax.rem(lax.axis_index("seq"), ways)
    share = tokens // ways
    per = share * heads
    pick = eye(STAT_ROWS, head_dim)
    for way, out_ref in enumerate(out_refs):
        first = lax.bitwise_xor(here, way) * share
        out_ref[:per, :] = rows_buf[pl.ds(first, share)].reshape(per, head_dim)
        turned = dot_rows(pick, stat_buf[pl.ds(first, share)].reshape(per, head_dim)).astype(BF16)
        for at in range(per // LANES):
            start = per + at * STAT_ROWS
            out_ref[start : start + STAT_ROWS, :] = turned[:, at * LANES : (at + 1) * LANES]


def attend(length, query, place, blocks, score_scale, ways):
    tokens, heads, head_dim = query.shape
    kv_count = place.shape[0]
    group = heads // kv_count
    per = tokens * heads // ways
    piece = jax.ShapeDtypeStruct((per + per // LANES * STAT_ROWS, head_dim), BF16)
    return pl.pallas_call(
        functools.partial(attend_kernel, score_scale, ways),
        out_shape=(piece,) * ways,
        in_specs=[SMEM] + [VMEM] * (2 + len(blocks)),
        out_specs=(VMEM,) * ways,
        scratch_shapes=[
            pltpu.VMEM((tokens, kv_count, group, head_dim), BF16),
            pltpu.VMEM((tokens, kv_count, group, head_dim), BF16),
        ],
        compiler_params=PARAMS,
        name="attend",
    )(length, query, place, *blocks)


def fresh_kernel(
    score_scale, ways, query_ref, keys_hbm, values_hbm, depth_hbm, out_ref, keys_ref, values_ref, depth_ref, sems
):
    copies = [
        pltpu.make_async_copy(source, target, sems.at[at])
        for at, (source, target) in enumerate(
            ((keys_hbm, keys_ref), (values_hbm, values_ref), (depth_hbm, depth_ref))
        )
    ]
    for copy in copies:
        copy.start()
    tokens, heads, head_dim = query_ref.shape
    kv_count = keys_ref.shape[0] // tokens
    share = tokens // ways
    per = share * heads
    first = lax.rem(lax.axis_index("seq"), ways) * share
    shape = (per, tokens * kv_count)
    _, own = split_off(lax.broadcasted_iota(jnp.int32, shape, 0), heads // kv_count)
    own_kv, own_token = split_off(own, kv_count)
    new_kv, new_token = split_off(lax.broadcasted_iota(jnp.int32, (1, shape[1]), 1), kv_count)
    for copy in copies:
        copy.wait()
    new_depth = jnp.zeros_like(new_token)
    for t in range(tokens):
        new_depth = jnp.where(new_token == t, depth_ref[t], new_depth)
    own_depth = jnp.zeros_like(own_token)
    for t in range(share):
        own_depth = jnp.where(own_token == t, depth_ref[first + t], own_depth)
    seen = (new_depth <= own_depth) & (new_kv == own_kv)
    query = query_ref[pl.ds(first, share)].reshape(per, head_dim)
    scores = dot_rows(query, keys_ref[...]) * score_scale + jnp.where(seen, 0.0, DEAD)
    peak, total, weighted = softmax_parts(scores, values_ref[...])
    out_ref[:per, :] = weighted
    stats = stat_lanes(peak, total, head_dim)
    row = lax.broadcasted_iota(jnp.int32, (WIDE_ROWS, LANES), 0)
    for at in range(per // LANES):
        turned = dot_rows(eye(STAT_ROWS, head_dim), stats[at * LANES : (at + 1) * LANES])
        peaks = turned[0:1] + turned[1:2] + turned[2:3]
        totals = turned[3:4] + turned[4:5] + turned[5:6]
        start = per + at * WIDE_ROWS
        out_ref[start : start + WIDE_ROWS, :] = jnp.where(row == 0, peaks, totals)


def fresh_rows(query, new_keys, new_values, depth, score_scale, ways):
    tokens, heads, head_dim = query.shape
    per = tokens * heads // ways
    flat = (new_keys.shape[0] * new_keys.shape[1], head_dim)
    inputs = [
        pltpu.with_memory_space_constraint(x, pltpu.HBM)
        for x in (new_keys.reshape(flat), new_values.reshape(flat), depth)
    ]
    return pl.pallas_call(
        functools.partial(fresh_kernel, score_scale, ways),
        out_shape=jax.ShapeDtypeStruct((per + per // LANES * WIDE_ROWS, head_dim), F32),
        in_specs=[VMEM, HBM, HBM, HBM],
        out_specs=VMEM,
        scratch_shapes=[
            pltpu.VMEM(flat, BF16),
            pltpu.VMEM(flat, BF16),
            pltpu.SMEM(depth.shape, jnp.int32),
            pltpu.SemaphoreType.DMA((3,)),
        ],
        compiler_params=PARAMS,
        name="fresh",
    )(query, *inputs)


def tree(combine, parts):
    while len(parts) > 1:
        pairs = [combine(parts[k], parts[k + 1]) for k in range(0, len(parts) - 1, 2)]
        parts = pairs + parts[len(parts) & ~1 :]
    return parts[0]


def merge_kernel(per, last, *refs):
    *in_refs, out_ref = refs
    head_dim = out_ref.shape[1]
    chunks = per // LANES
    turn = eye(LANES, LANES)
    factor_rows = -(-3 * len(in_refs) // STAT_ROWS) * STAT_ROWS
    for at in range(chunks):
        peaks, totals = [], []
        for ref in in_refs:
            rows_in = (ref.shape[0] - per) // chunks
            stats = ref[per + at * rows_in : per + (at + 1) * rows_in, :].astype(F32)
            if ref.dtype == BF16:
                peaks.append(stats[0:1] + stats[1:2] + stats[2:3])
                totals.append(stats[3:4] + stats[4:5] + stats[5:6])
            else:
                peaks.append(stats[0:1])
                totals.append(stats[1:2])
        peak = tree(jnp.maximum, peaks)
        factors = [jnp.exp(p - peak) for p in peaks]
        total = tree(jnp.add, [f * t for f, t in zip(factors, totals)])
        if last:
            factors = [f / total for f in factors]
        else:
            start = per + at * WIDE_ROWS
            row = lax.broadcasted_iota(jnp.int32, (WIDE_ROWS, LANES), 0)
            out_ref[start : start + WIDE_ROWS, :] = jnp.where(row == 0, peak, total)
        parts = [part for f in factors for part in three_parts(f)]
        columns = dot_rows(turn, stacked(parts, (factor_rows, LANES)))
        terms = []
        for k, ref in enumerate(in_refs):
            column = columns[:, 3 * k : 3 * k + 1] + columns[:, 3 * k + 1 : 3 * k + 2]
            column = jnp.broadcast_to(column + columns[:, 3 * k + 2 : 3 * k + 3], (LANES, head_dim))
            terms.append(ref[at * LANES : (at + 1) * LANES, :].astype(F32) * column)
        out_ref[at * LANES : (at + 1) * LANES, :] = tree(jnp.add, terms).astype(out_ref.dtype)


def merge(states, per, last):
    head_dim = states[0].shape[1]
    if last:
        out = jax.ShapeDtypeStruct((per, head_dim), BF16)
    else:
        out = jax.ShapeDtypeStruct((per + per // LANES * WIDE_ROWS, head_dim), F32)
    return pl.pallas_call(
        functools.partial(merge_kernel, per, last),
        out_shape=out,
        in_specs=[VMEM] * len(states),
        out_specs=VMEM,
        compiler_params=PARAMS,
        name="merge",
    )(*states)


def join_kernel(*refs):
    *in_refs, out_ref, sems = refs
    ways = len(in_refs)
    per = in_refs[0].shape[0]
    here = lax.rem(lax.axis_index("seq"), ways)
    copies = []
    for way, ref in enumerate(in_refs):
        start = pl.multiple_of(lax.bitwise_xor(here, way) * per, per)
        copies.append(pltpu.make_async_copy(ref, out_ref.at[pl.ds(start, per)], sems.at[way]))
        copies[-1].start()
    for copy in copies:
        copy.wait()


def join(pieces):
    per, head_dim = pieces[0].shape
    return pl.pallas_call(
        join_kernel,
        out_shape=jax.ShapeDtypeStruct((len(pieces) * per, head_dim), BF16),
        in_specs=[VMEM] * len(pieces),
        out_specs=HBM,
        scratch_shapes=[pltpu.SemaphoreType.DMA((len(pieces),))],
        compiler_params=PARAMS,
        name="join",
    )(*pieces)


def relay_kernel(kv_count, slots_hbm, length_ref, got_ref, keys_ref, values_ref, slots_ref, sem):
    copy = pltpu.make_async_copy(slots_hbm, slots_ref, sem)
    copy.start()
    copy.wait()
    slot_count, span, head_dim = keys_ref.shape
    row = lax.broadcasted_iota(jnp.int32, (span, head_dim), 0)
    live = length_ref[0] * kv_count - lax.axis_index("seq") * (slot_count * span)

    def one(t, carry):
        slot = slots_ref[t]
        kept = row < live - t * span
        for c, out_ref in enumerate((keys_ref, values_ref)):
            block = got_ref[slot // 2, c, slot % 2].astype(F32)
            out_ref[t] = jnp.where(kept, block, 0.0).astype(BF16)
        return carry

    lax.fori_loop(0, slot_count, one, 0, unroll=4)


def relay(span_slots, prompt_length, got, kv_count):
    _, _, _, span, head_dim = got.shape
    shape = jax.ShapeDtypeStruct((span_slots.shape[0], span, head_dim), BF16)
    return pl.pallas_call(
        functools.partial(relay_kernel, kv_count),
        out_shape=(shape, shape),
        in_specs=[HBM, SMEM, VMEM],
        out_specs=(VMEM, VMEM),
        scratch_shapes=[pltpu.SMEM(span_slots.shape, jnp.int32), pltpu.SemaphoreType.DMA],
        compiler_params=PARAMS,
        name="relay",
    )(pltpu.with_memory_space_constraint(span_slots, pltpu.HBM), prompt_length, got)


def step(
    cache_keys,
    cache_values,
    span_slots,
    prompt_length,
    queries,
    new_keys,
    new_values,
    decode_offsets,
):
    row_count, kv_all, head_dim = cache_keys.shape
    seq_count = lax.axis_size("seq")
    head_count = lax.axis_size("head")
    cycle_size = seq_count * head_count
    slot_count = span_slots.shape[0]
    span_rows = row_count // (2 * seq_count)
    kv_local = kv_all // head_count
    token_count, heads, _ = queries.shape
    score_scale = 1.0 / math.sqrt(head_dim)
    shard_rows = slot_count * span_rows
    ways = math.gcd(4, seq_count)

    packed, mine, away, place, query = pack(
        cache_keys, cache_values, span_slots, queries, seq_count, head_count
    )
    flat = (2, row_count * kv_local, head_dim)
    blocks = [mine.reshape(flat)]
    for shift in range(1, head_count):
        blocks.append(
            lax.ppermute(
                away[shift - 1].reshape(flat),
                "head",
                [(h, (h + shift) % head_count) for h in range(head_count)],
            )
        )
    got = lax.all_to_all(
        packed.reshape(cycle_size, 2, 2 * span_rows * kv_local, head_dim),
        ("head", "seq"),
        split_axis=0,
        concat_axis=0,
        tiled=True,
    )

    pieces = attend(prompt_length, query, place, blocks, score_scale, ways)
    per = token_count * heads // ways

    def swapped(x, distance):
        return lax.ppermute(x, "seq", [(s, s ^ distance) for s in range(seq_count)])

    states = [pieces[0]] + [swapped(pieces[way], way) for way in range(1, ways)]
    fresh = fresh_rows(query, new_keys, new_values, decode_offsets, score_scale, ways)
    distance = ways
    while distance < seq_count:
        state = merge(states, per, False)
        states = [state, swapped(state, distance)]
        distance *= 2
    state = merge(states + [fresh], per, True)
    finished = [state] + [swapped(state, way) for way in range(1, ways)]
    attended = join(finished)

    relaid_keys, relaid_values = relay(
        span_slots,
        prompt_length,
        got.reshape(cycle_size, 2, 2, span_rows * kv_local, head_dim),
        kv_local,
    )
    whole = (shard_rows, kv_local, head_dim)
    return (
        relaid_keys.reshape(whole),
        relaid_values.reshape(whole),
        attended.reshape(token_count, heads, head_dim),
    )


def solution(mesh):
    return jax.shard_map(
        step,
        mesh=mesh,
        in_specs=(
            P(("rep", "head", "seq"), None, None),
            P(("rep", "head", "seq"), None, None),
            P("rep"),
            P("rep"),
            P("rep", "head", None),
            P("rep", "head", None),
            P("rep", "head", None),
            P("rep"),
        ),
        out_specs=(
            P(("rep", "seq"), "head", None),
            P(("rep", "seq"), "head", None),
            P("rep", "head", None),
        ),
        check_vma=False,
    )
```

```python
import functools
import math

import jax
import jax.numpy as jnp
from jax import lax
from jax.experimental import pallas as pl
from jax.experimental.pallas import tpu as pltpu
from jax.sharding import PartitionSpec as P


BF16 = jnp.bfloat16
F32 = jnp.float32
DEAD = -1e30
STAT_ROWS = 16
WIDE_ROWS = 8
LANES = 128
VMEM = pl.BlockSpec(memory_space=pltpu.VMEM)
SMEM = pl.BlockSpec(memory_space=pltpu.SMEM)
HBM = pl.BlockSpec(memory_space=pltpu.HBM)
PARAMS = pltpu.CompilerParams(vmem_limit_bytes=16 * 1024 * 1024)


def dot_rows(a, b):
    return lax.dot_general(a, b, (((1,), (1,)), ((), ())), preferred_element_type=F32)


def three_parts(x):
    high = x.astype(BF16).astype(F32)
    rest = x - high
    middle = rest.astype(BF16).astype(F32)
    return [high, middle, rest - middle]


def stacked(parts, like):
    row = lax.broadcasted_iota(jnp.int32, like, 0)
    out = jnp.zeros(like, F32)
    for at, part in enumerate(parts):
        out = jnp.where(row == at, part, out)
    return out.astype(BF16)


def eye(rows, columns):
    return (
        lax.broadcasted_iota(jnp.int32, (rows, columns), 0)
        == lax.broadcasted_iota(jnp.int32, (rows, columns), 1)
    ).astype(F32).astype(BF16)


def split_off(x, n):
    if n & (n - 1) == 0:
        return x & (n - 1), x >> (n.bit_length() - 1)
    return lax.rem(x, n), lax.div(x, n)


def place_of(index, ways):
    return lax.rem(lax.bitwise_xor(index, lax.div(lax.rem(index, 2 * ways), ways) * (ways // 2)), ways)


def hop_distance(distance, ways):
    return distance + ways // 2 if distance == ways else distance


def pack_kernel(
    span_rows,
    keys_ref,
    values_ref,
    slots_hbm,
    query_hbm,
    send_ref,
    mine_ref,
    away_ref,
    place_ref,
    query_ref,
    slots_ref,
    in_sems,
    out_sems,
    sems,
):
    seq_count, _, head_count, _, _ = keys_ref.shape
    slot_count = slots_hbm.shape[0]
    me = lax.axis_index("head")
    seq_index = lax.axis_index("seq")
    facts = pltpu.make_async_copy(slots_hbm, slots_ref, sems.at[0])
    facts.start()
    staged = pltpu.make_async_copy(query_hbm, query_ref, sems.at[1])
    blocks = []
    for shift in list(range(1, head_count)) + [0]:
        h = lax.rem(me + shift, head_count)
        for c, source in enumerate((keys_ref, values_ref)):
            target = away_ref.at[shift - 1, c] if shift else mine_ref.at[c]
            copy = pltpu.make_async_copy(source.at[:, :, h], target, in_sems.at[shift, c])
            copy.start()
            out = pltpu.make_async_copy(target, send_ref.at[h, :, c], out_sems.at[shift, c])
            blocks.append((copy, out))
    staged.start()
    for copy, out in blocks:
        copy.wait()
        out.start()
    facts.wait()

    wanted = []
    for b in range(head_count):
        first = 2 * (lax.rem(me + head_count - b, head_count) * seq_count + seq_index)
        wanted += [first, first + 1]

    def look(t, places):
        slot = slots_ref[t]
        return tuple(jnp.where(slot == w, t, p) for w, p in zip(wanted, places))

    places = lax.fori_loop(0, slot_count, look, tuple(jnp.int32(0) for _ in wanted))
    column = lax.broadcasted_iota(jnp.int32, (1, place_ref.shape[1]), 1)
    row, rest = split_off(column, span_rows)
    half, rest = split_off(rest, 2)
    turn, block = split_off(rest, seq_count)
    span = jnp.zeros_like(column)
    for at, place in enumerate(places):
        span = jnp.where(2 * block + half == at, place, span)
    place_ref[...] = (turn * slot_count + span) * span_rows + row
    for _, out in blocks:
        out.wait()
    staged.wait()


def pack(cache_keys, cache_values, span_slots, queries, seq_count, head_count):
    row_count, kv_all, head_dim = cache_keys.shape
    kv = kv_all // head_count
    rows = row_count // seq_count
    split = (seq_count, rows, head_count, kv, head_dim)
    block = (seq_count, rows, kv, head_dim)
    inputs = [
        pltpu.with_memory_space_constraint(x, pltpu.HBM)
        for x in (cache_keys.reshape(split), cache_values.reshape(split), span_slots, queries)
    ]
    return pl.pallas_call(
        functools.partial(pack_kernel, rows // 2),
        out_shape=(
            jax.ShapeDtypeStruct((head_count, seq_count, 2, rows, kv, head_dim), BF16),
            jax.ShapeDtypeStruct((2,) + block, BF16),
            jax.ShapeDtypeStruct((head_count - 1, 2) + block, BF16),
            jax.ShapeDtypeStruct((1, head_count * row_count), jnp.int32),
            jax.ShapeDtypeStruct(queries.shape, BF16),
        ),
        in_specs=[HBM] * len(inputs),
        out_specs=(HBM,) + (VMEM,) * 4,
        scratch_shapes=[
            pltpu.SMEM(span_slots.shape, jnp.int32),
            pltpu.SemaphoreType.DMA((head_count, 2)),
            pltpu.SemaphoreType.DMA((head_count, 2)),
            pltpu.SemaphoreType.DMA((2,)),
        ],
        compiler_params=PARAMS,
        name="pack",
    )(*inputs)


def softmax_parts(scores, values):
    peak = jnp.max(scores, axis=1, keepdims=True)
    weights = jnp.exp(scores - peak)
    total = jnp.sum(weights, axis=1, keepdims=True)
    weighted = jnp.dot(weights.astype(BF16), values, preferred_element_type=F32)
    return peak, total, weighted


def stat_lanes(peak, total, head_dim):
    lane = lax.broadcasted_iota(jnp.int32, (peak.shape[0], head_dim), 1)
    stats = jnp.zeros((peak.shape[0], head_dim), F32)
    for at, part in enumerate(three_parts(peak) + three_parts(total)):
        stats = jnp.where(lane == at, part, stats)
    return stats.astype(BF16)


def attend_kernel(score_scale, ways, length_ref, query_ref, place_ref, *rest):
    *block_refs, rows_buf, stat_buf, wide_buf = rest
    block_refs, out_refs = block_refs[:-ways], block_refs[-ways:]
    tokens, heads, head_dim = query_ref.shape
    kv_count = rows_buf.shape[1]
    group = heads // kv_count
    stored = block_refs[0].shape[1]
    for at, ref in enumerate(block_refs):
        for c in range(2):
            wide_buf[c, at * stored : (at + 1) * stored, :] = ref[c].astype(F32)
    columns = place_ref.shape[1]
    bias = jnp.where(place_ref[...] < length_ref[0], 0.0, DEAD)
    for g in range(kv_count):
        query = query_ref[:, g * group : (g + 1) * group, :].reshape(tokens * group, head_dim)
        own = pl.ds(g, columns, stride=kv_count)
        keys = wide_buf[0, own, :].astype(BF16)
        values = wide_buf[1, own, :].astype(BF16)
        peak, total, weighted = softmax_parts(dot_rows(query, keys) * score_scale + bias, values)
        rows_buf[:, g] = weighted.astype(BF16).reshape(tokens, group, head_dim)
        stat_buf[:, g] = stat_lanes(peak, total, head_dim).reshape(tokens, group, head_dim)
    here = place_of(lax.axis_index("seq"), ways)
    share = tokens // ways
    per = share * heads
    pick = eye(STAT_ROWS, head_dim)
    for way, out_ref in enumerate(out_refs):
        first = lax.bitwise_xor(here, way) * share
        out_ref[:per, :] = rows_buf[pl.ds(first, share)].reshape(per, head_dim)
        turned = dot_rows(pick, stat_buf[pl.ds(first, share)].reshape(per, head_dim)).astype(BF16)
        for at in range(per // LANES):
            start = per + at * STAT_ROWS
            out_ref[start : start + STAT_ROWS, :] = turned[:, at * LANES : (at + 1) * LANES]


def attend(length, query, place, blocks, score_scale, ways):
    tokens, heads, head_dim = query.shape
    rows = sum(block.shape[1] for block in blocks)
    kv_count = rows // place.shape[1]
    group = heads // kv_count
    per = tokens * heads // ways
    piece = jax.ShapeDtypeStruct((per + per // LANES * STAT_ROWS, head_dim), BF16)
    return pl.pallas_call(
        functools.partial(attend_kernel, score_scale, ways),
        out_shape=(piece,) * ways,
        in_specs=[SMEM] + [VMEM] * (2 + len(blocks)),
        out_specs=(VMEM,) * ways,
        scratch_shapes=[
            pltpu.VMEM((tokens, kv_count, group, head_dim), BF16),
            pltpu.VMEM((tokens, kv_count, group, head_dim), BF16),
            pltpu.VMEM((2, rows, head_dim), F32),
        ],
        compiler_params=PARAMS,
        name="attend",
    )(length, query, place, *blocks)


def fresh_kernel(
    score_scale, ways, query_ref, keys_hbm, values_hbm, depth_hbm, out_ref, keys_ref, values_ref, depth_ref, sems
):
    copies = [
        pltpu.make_async_copy(source, target, sems.at[at])
        for at, (source, target) in enumerate(
            ((keys_hbm, keys_ref), (values_hbm, values_ref), (depth_hbm, depth_ref))
        )
    ]
    for copy in copies:
        copy.start()
    tokens, heads, head_dim = query_ref.shape
    kv_count = keys_ref.shape[0] // tokens
    share = tokens // ways
    per = share * heads
    first = place_of(lax.axis_index("seq"), ways) * share
    shape = (per, tokens * kv_count)
    _, own = split_off(lax.broadcasted_iota(jnp.int32, shape, 0), heads // kv_count)
    own_kv, own_token = split_off(own, kv_count)
    new_kv, new_token = split_off(lax.broadcasted_iota(jnp.int32, (1, shape[1]), 1), kv_count)
    for copy in copies:
        copy.wait()
    new_depth = jnp.zeros_like(new_token)
    for t in range(tokens):
        new_depth = jnp.where(new_token == t, depth_ref[t], new_depth)
    own_depth = jnp.zeros_like(own_token)
    for t in range(share):
        own_depth = jnp.where(own_token == t, depth_ref[first + t], own_depth)
    seen = (new_depth <= own_depth) & (new_kv == own_kv)
    query = query_ref[pl.ds(first, share)].reshape(per, head_dim)
    scores = dot_rows(query, keys_ref[...]) * score_scale + jnp.where(seen, 0.0, DEAD)
    peak, total, weighted = softmax_parts(scores, values_ref[...])
    out_ref[:per, :] = weighted
    stats = stat_lanes(peak, total, head_dim)
    row = lax.broadcasted_iota(jnp.int32, (WIDE_ROWS, LANES), 0)
    for at in range(per // LANES):
        turned = dot_rows(eye(STAT_ROWS, head_dim), stats[at * LANES : (at + 1) * LANES])
        peaks = turned[0:1] + turned[1:2] + turned[2:3]
        totals = turned[3:4] + turned[4:5] + turned[5:6]
        start = per + at * WIDE_ROWS
        out_ref[start : start + WIDE_ROWS, :] = jnp.where(row == 0, peaks, totals)


def fresh_rows(query, new_keys, new_values, depth, score_scale, ways):
    tokens, heads, head_dim = query.shape
    per = tokens * heads // ways
    flat = (new_keys.shape[0] * new_keys.shape[1], head_dim)
    inputs = [
        pltpu.with_memory_space_constraint(x, pltpu.HBM)
        for x in (new_keys.reshape(flat), new_values.reshape(flat), depth)
    ]
    return pl.pallas_call(
        functools.partial(fresh_kernel, score_scale, ways),
        out_shape=jax.ShapeDtypeStruct((per + per // LANES * WIDE_ROWS, head_dim), F32),
        in_specs=[VMEM, HBM, HBM, HBM],
        out_specs=VMEM,
        scratch_shapes=[
            pltpu.VMEM(flat, BF16),
            pltpu.VMEM(flat, BF16),
            pltpu.SMEM(depth.shape, jnp.int32),
            pltpu.SemaphoreType.DMA((3,)),
        ],
        compiler_params=PARAMS,
        name="fresh",
    )(query, *inputs)


def tree(combine, parts):
    while len(parts) > 1:
        pairs = [combine(parts[k], parts[k + 1]) for k in range(0, len(parts) - 1, 2)]
        parts = pairs + parts[len(parts) & ~1 :]
    return parts[0]


def merge_kernel(per, last, *refs):
    *in_refs, out_ref = refs
    head_dim = out_ref.shape[1]
    chunks = per // LANES
    turn = eye(LANES, LANES)
    factor_rows = -(-3 * len(in_refs) // STAT_ROWS) * STAT_ROWS
    for at in range(chunks):
        peaks, totals = [], []
        for ref in in_refs:
            rows_in = (ref.shape[0] - per) // chunks
            stats = ref[per + at * rows_in : per + (at + 1) * rows_in, :].astype(F32)
            if ref.dtype == BF16:
                peaks.append(stats[0:1] + stats[1:2] + stats[2:3])
                totals.append(stats[3:4] + stats[4:5] + stats[5:6])
            else:
                peaks.append(stats[0:1])
                totals.append(stats[1:2])
        peak = tree(jnp.maximum, peaks)
        factors = [jnp.exp(p - peak) for p in peaks]
        total = tree(jnp.add, [f * t for f, t in zip(factors, totals)])
        if last:
            factors = [f / total for f in factors]
        else:
            start = per + at * STAT_ROWS
            out_ref[start : start + STAT_ROWS, :] = stacked(
                three_parts(peak) + three_parts(total), (STAT_ROWS, LANES)
            )
        parts = [part for f in factors for part in three_parts(f)]
        columns = dot_rows(turn, stacked(parts, (factor_rows, LANES)))
        terms = []
        for k, ref in enumerate(in_refs):
            column = columns[:, 3 * k : 3 * k + 1] + columns[:, 3 * k + 1 : 3 * k + 2]
            column = jnp.broadcast_to(column + columns[:, 3 * k + 2 : 3 * k + 3], (LANES, head_dim))
            terms.append(ref[at * LANES : (at + 1) * LANES, :].astype(F32) * column)
        out_ref[at * LANES : (at + 1) * LANES, :] = tree(jnp.add, terms).astype(out_ref.dtype)


def merge(states, per, last):
    head_dim = states[0].shape[1]
    if last:
        out = jax.ShapeDtypeStruct((per, head_dim), BF16)
    else:
        out = jax.ShapeDtypeStruct((per + per // LANES * STAT_ROWS, head_dim), BF16)
    return pl.pallas_call(
        functools.partial(merge_kernel, per, last),
        out_shape=out,
        in_specs=[VMEM] * len(states),
        out_specs=VMEM,
        compiler_params=PARAMS,
        name="merge",
    )(*states)


def join_kernel(*refs):
    *in_refs, out_ref, sems = refs
    ways = len(in_refs)
    per = in_refs[0].shape[0]
    here = place_of(lax.axis_index("seq"), ways)
    copies = []
    for way, ref in enumerate(in_refs):
        start = pl.multiple_of(lax.bitwise_xor(here, way) * per, per)
        copies.append(pltpu.make_async_copy(ref, out_ref.at[pl.ds(start, per)], sems.at[way]))
        copies[-1].start()
    for copy in copies:
        copy.wait()


def join(pieces):
    per, head_dim = pieces[0].shape
    return pl.pallas_call(
        join_kernel,
        out_shape=jax.ShapeDtypeStruct((len(pieces) * per, head_dim), BF16),
        in_specs=[VMEM] * len(pieces),
        out_specs=HBM,
        scratch_shapes=[pltpu.SemaphoreType.DMA((len(pieces),))],
        compiler_params=PARAMS,
        name="join",
    )(*pieces)


def relay_kernel(kv_count, slots_hbm, length_ref, got_ref, keys_ref, values_ref, slots_ref, sem):
    copy = pltpu.make_async_copy(slots_hbm, slots_ref, sem)
    copy.start()
    copy.wait()
    slot_count, span, head_dim = keys_ref.shape
    row = lax.broadcasted_iota(jnp.int32, (span, head_dim), 0)
    live = length_ref[0] * kv_count - lax.axis_index("seq") * (slot_count * span)

    def one(t, carry):
        slot = slots_ref[t]
        kept = row < live - t * span
        for c, out_ref in enumerate((keys_ref, values_ref)):
            block = got_ref[slot // 2, c, slot % 2].astype(F32)
            out_ref[t] = jnp.where(kept, block, 0.0).astype(BF16)
        return carry

    lax.fori_loop(0, slot_count, one, 0, unroll=4)


def relay(span_slots, prompt_length, got, kv_count):
    _, _, _, span, head_dim = got.shape
    shape = jax.ShapeDtypeStruct((span_slots.shape[0], span, head_dim), BF16)
    return pl.pallas_call(
        functools.partial(relay_kernel, kv_count),
        out_shape=(shape, shape),
        in_specs=[HBM, SMEM, VMEM],
        out_specs=(VMEM, VMEM),
        scratch_shapes=[pltpu.SMEM(span_slots.shape, jnp.int32), pltpu.SemaphoreType.DMA],
        compiler_params=PARAMS,
        name="relay",
    )(pltpu.with_memory_space_constraint(span_slots, pltpu.HBM), prompt_length, got)


def step(
    cache_keys,
    cache_values,
    span_slots,
    prompt_length,
    queries,
    new_keys,
    new_values,
    decode_offsets,
):
    row_count, kv_all, head_dim = cache_keys.shape
    seq_count = lax.axis_size("seq")
    head_count = lax.axis_size("head")
    cycle_size = seq_count * head_count
    slot_count = span_slots.shape[0]
    span_rows = row_count // (2 * seq_count)
    kv_local = kv_all // head_count
    token_count, heads, _ = queries.shape
    score_scale = 1.0 / math.sqrt(head_dim)
    shard_rows = slot_count * span_rows
    ways = math.gcd(4, seq_count)

    packed, mine, away, place, query = pack(
        cache_keys, cache_values, span_slots, queries, seq_count, head_count
    )
    flat = (2, row_count * kv_local, head_dim)
    blocks = [mine.reshape(flat)]
    for shift in range(1, head_count):
        blocks.append(
            lax.ppermute(
                away[shift - 1].reshape(flat),
                "head",
                [(h, (h + shift) % head_count) for h in range(head_count)],
            )
        )
    got = lax.all_to_all(
        packed.reshape(cycle_size, 2, 2 * span_rows * kv_local, head_dim),
        ("head", "seq"),
        split_axis=0,
        concat_axis=0,
        tiled=True,
    )

    pieces = attend(prompt_length, query, place, blocks, score_scale, ways)
    per = token_count * heads // ways

    def swapped(x, distance):
        return lax.ppermute(x, "seq", [(s, s ^ distance) for s in range(seq_count)])

    states = [pieces[0]]
    for way in range(1, ways):
        states.append(swapped(pieces[way], way))
    fresh = fresh_rows(query, new_keys, new_values, decode_offsets, score_scale, ways)
    distance = ways
    while distance < seq_count:
        state = merge(states, per, False)
        states = [state, swapped(state, hop_distance(distance, ways))]
        distance *= 2
    state = merge(states + [fresh], per, True)
    finished = [state]
    for way in range(1, ways):
        finished.append(swapped(state, way))
    attended = join(finished)

    relaid_keys, relaid_values = relay(
        span_slots,
        prompt_length,
        got.reshape(cycle_size, 2, 2, span_rows * kv_local, head_dim),
        kv_local,
    )
    whole = (shard_rows, kv_local, head_dim)
    return (
        relaid_keys.reshape(whole),
        relaid_values.reshape(whole),
        attended.reshape(token_count, heads, head_dim),
    )


def solution(mesh):
    return jax.shard_map(
        step,
        mesh=mesh,
        in_specs=(
            P(("rep", "head", "seq"), None, None),
            P(("rep", "head", "seq"), None, None),
            P("rep"),
            P("rep"),
            P("rep", "head", None),
            P("rep", "head", None),
            P("rep", "head", None),
            P("rep"),
        ),
        out_specs=(
            P(("rep", "seq"), "head", None),
            P(("rep", "seq"), "head", None),
            P("rep", "head", None),
        ),
        check_vma=False,
    )
```

```python
import functools
import math

import jax
import jax.numpy as jnp
from jax import lax
from jax.experimental import pallas as pl
from jax.experimental.pallas import tpu as pltpu
from jax.sharding import PartitionSpec as P


BF16 = jnp.bfloat16
F32 = jnp.float32
DEAD = -1e30
STAT_ROWS = 8
WIDE_ROWS = 8
LANES = 128
VMEM = pl.BlockSpec(memory_space=pltpu.VMEM)
SMEM = pl.BlockSpec(memory_space=pltpu.SMEM)
HBM = pl.BlockSpec(memory_space=pltpu.HBM)
PARAMS = pltpu.CompilerParams(vmem_limit_bytes=16 * 1024 * 1024)


def dot_rows(a, b):
    return lax.dot_general(a, b, (((1,), (1,)), ((), ())), preferred_element_type=F32)


def three_parts(x):
    high = x.astype(BF16).astype(F32)
    rest = x - high
    middle = rest.astype(BF16).astype(F32)
    return [high, middle, rest - middle]


def stacked(parts, like):
    row = lax.broadcasted_iota(jnp.int32, like, 0)
    out = jnp.zeros(like, F32)
    for at, part in enumerate(parts):
        out = jnp.where(row == at, part, out)
    return out.astype(BF16)


def eye(rows, columns):
    return (
        lax.broadcasted_iota(jnp.int32, (rows, columns), 0)
        == lax.broadcasted_iota(jnp.int32, (rows, columns), 1)
    ).astype(F32).astype(BF16)


def split_off(x, n):
    if n & (n - 1) == 0:
        return x & (n - 1), x >> (n.bit_length() - 1)
    return lax.rem(x, n), lax.div(x, n)


def place_of(index, ways):
    return lax.rem(lax.bitwise_xor(index, lax.div(lax.rem(index, 2 * ways), ways) * (ways // 2)), ways)


def hop_distance(distance, ways):
    return distance + ways // 2 if distance == ways else distance


def pack_kernel(
    span_rows,
    keys_ref,
    values_ref,
    slots_hbm,
    query_hbm,
    send_ref,
    mine_ref,
    away_ref,
    place_ref,
    query_ref,
    slots_ref,
    in_sems,
    out_sems,
    sems,
):
    seq_count, _, head_count, _, _ = keys_ref.shape
    slot_count = slots_hbm.shape[0]
    me = lax.axis_index("head")
    seq_index = lax.axis_index("seq")
    facts = pltpu.make_async_copy(slots_hbm, slots_ref, sems.at[0])
    facts.start()
    staged = pltpu.make_async_copy(query_hbm, query_ref, sems.at[1])
    blocks = []
    for shift in list(range(1, head_count)) + [0]:
        h = lax.rem(me + shift, head_count)
        for c, source in enumerate((keys_ref, values_ref)):
            target = away_ref.at[shift - 1, c] if shift else mine_ref.at[c]
            copy = pltpu.make_async_copy(source.at[:, :, h], target, in_sems.at[shift, c])
            copy.start()
            out = pltpu.make_async_copy(target, send_ref.at[h, :, c], out_sems.at[shift, c])
            blocks.append((copy, out))
    staged.start()
    for copy, out in blocks:
        copy.wait()
        out.start()
    facts.wait()

    wanted = []
    for b in range(head_count):
        first = 2 * (lax.rem(me + head_count - b, head_count) * seq_count + seq_index)
        wanted += [first, first + 1]

    def look(t, places):
        slot = slots_ref[t]
        return tuple(jnp.where(slot == w, t, p) for w, p in zip(wanted, places))

    places = lax.fori_loop(0, slot_count, look, tuple(jnp.int32(0) for _ in wanted))
    column = lax.broadcasted_iota(jnp.int32, (1, place_ref.shape[1]), 1)
    row, rest = split_off(column, span_rows)
    half, rest = split_off(rest, 2)
    turn, block = split_off(rest, seq_count)
    span = jnp.zeros_like(column)
    for at, place in enumerate(places):
        span = jnp.where(2 * block + half == at, place, span)
    place_ref[...] = (turn * slot_count + span) * span_rows + row
    for _, out in blocks:
        out.wait()
    staged.wait()


def pack(cache_keys, cache_values, span_slots, queries, seq_count, head_count):
    row_count, kv_all, head_dim = cache_keys.shape
    kv = kv_all // head_count
    rows = row_count // seq_count
    split = (seq_count, rows, head_count, kv, head_dim)
    block = (seq_count, rows, kv, head_dim)
    inputs = [
        pltpu.with_memory_space_constraint(x, pltpu.HBM)
        for x in (cache_keys.reshape(split), cache_values.reshape(split), span_slots, queries)
    ]
    return pl.pallas_call(
        functools.partial(pack_kernel, rows // 2),
        out_shape=(
            jax.ShapeDtypeStruct((head_count, seq_count, 2, rows, kv, head_dim), BF16),
            jax.ShapeDtypeStruct((2,) + block, BF16),
            jax.ShapeDtypeStruct((head_count - 1, 2) + block, BF16),
            jax.ShapeDtypeStruct((1, head_count * row_count), jnp.int32),
            jax.ShapeDtypeStruct(queries.shape, BF16),
        ),
        in_specs=[HBM] * len(inputs),
        out_specs=(HBM,) + (VMEM,) * 4,
        scratch_shapes=[
            pltpu.SMEM(span_slots.shape, jnp.int32),
            pltpu.SemaphoreType.DMA((head_count, 2)),
            pltpu.SemaphoreType.DMA((head_count, 2)),
            pltpu.SemaphoreType.DMA((2,)),
        ],
        compiler_params=PARAMS,
        name="pack",
    )(*inputs)


def softmax_parts(scores, values):
    peak = jnp.max(scores, axis=1, keepdims=True)
    weights = jnp.exp(scores - peak)
    total = jnp.sum(weights, axis=1, keepdims=True)
    high = weights.astype(BF16)
    low = (weights - high.astype(F32)).astype(BF16)
    weighted = jnp.dot(high, values, preferred_element_type=F32)
    weighted = weighted + jnp.dot(low, values, preferred_element_type=F32)
    return peak, total, weighted


def stat_lanes(peak, total, head_dim):
    lane = lax.broadcasted_iota(jnp.int32, (peak.shape[0], head_dim), 1)
    stats = jnp.zeros((peak.shape[0], head_dim), F32)
    for at, part in enumerate(three_parts(peak) + three_parts(total)):
        stats = jnp.where(lane == at, part, stats)
    return stats.astype(BF16)


def attend_kernel(score_scale, ways, length_ref, query_ref, place_ref, *rest):
    *block_refs, rows_buf, stat_buf, wide_buf = rest
    block_refs, out_refs = block_refs[:-ways], block_refs[-ways:]
    tokens, heads, head_dim = query_ref.shape
    kv_count = rows_buf.shape[1]
    group = heads // kv_count
    stored = block_refs[0].shape[1]
    for at, ref in enumerate(block_refs):
        for c in range(2):
            wide_buf[c, at * stored : (at + 1) * stored, :] = ref[c].astype(F32)
    columns = place_ref.shape[1]
    bias = jnp.where(place_ref[...] < length_ref[0], 0.0, DEAD)
    for g in range(kv_count):
        query = query_ref[:, g * group : (g + 1) * group, :].reshape(tokens * group, head_dim)
        own = pl.ds(g, columns, stride=kv_count)
        keys = wide_buf[0, own, :].astype(BF16)
        values = wide_buf[1, own, :].astype(BF16)
        peak, total, weighted = softmax_parts(dot_rows(query, keys) * score_scale + bias, values)
        rows_buf[:, g] = weighted.astype(BF16).reshape(tokens, group, head_dim)
        stat_buf[:, g] = stat_lanes(peak, total, head_dim).reshape(tokens, group, head_dim)
    here = place_of(lax.axis_index("seq"), ways)
    share = tokens // ways
    per = share * heads
    pick = eye(STAT_ROWS, head_dim)
    for way, out_ref in enumerate(out_refs):
        first = lax.bitwise_xor(here, way) * share
        out_ref[:per, :] = rows_buf[pl.ds(first, share)].reshape(per, head_dim)
        turned = dot_rows(pick, stat_buf[pl.ds(first, share)].reshape(per, head_dim)).astype(BF16)
        for at in range(per // LANES):
            start = per + at * STAT_ROWS
            out_ref[start : start + STAT_ROWS, :] = turned[:, at * LANES : (at + 1) * LANES]


def attend(length, query, place, blocks, score_scale, ways):
    tokens, heads, head_dim = query.shape
    rows = sum(block.shape[1] for block in blocks)
    kv_count = rows // place.shape[1]
    group = heads // kv_count
    per = tokens * heads // ways
    piece = jax.ShapeDtypeStruct((per + per // LANES * STAT_ROWS, head_dim), BF16)
    return pl.pallas_call(
        functools.partial(attend_kernel, score_scale, ways),
        out_shape=(piece,) * ways,
        in_specs=[SMEM] + [VMEM] * (2 + len(blocks)),
        out_specs=(VMEM,) * ways,
        scratch_shapes=[
            pltpu.VMEM((tokens, kv_count, group, head_dim), BF16),
            pltpu.VMEM((tokens, kv_count, group, head_dim), BF16),
            pltpu.VMEM((2, rows, head_dim), F32),
        ],
        compiler_params=PARAMS,
        name="attend",
    )(length, query, place, *blocks)


def fresh_kernel(
    score_scale, ways, query_ref, keys_hbm, values_hbm, depth_hbm, out_ref, keys_ref, values_ref, depth_ref, sems
):
    copies = [
        pltpu.make_async_copy(source, target, sems.at[at])
        for at, (source, target) in enumerate(
            ((keys_hbm, keys_ref), (values_hbm, values_ref), (depth_hbm, depth_ref))
        )
    ]
    for copy in copies:
        copy.start()
    tokens, heads, head_dim = query_ref.shape
    kv_count = keys_ref.shape[0] // tokens
    share = tokens // ways
    per = share * heads
    first = place_of(lax.axis_index("seq"), ways) * share
    shape = (per, tokens * kv_count)
    _, own = split_off(lax.broadcasted_iota(jnp.int32, shape, 0), heads // kv_count)
    own_kv, own_token = split_off(own, kv_count)
    new_kv, new_token = split_off(lax.broadcasted_iota(jnp.int32, (1, shape[1]), 1), kv_count)
    for copy in copies:
        copy.wait()
    new_depth = jnp.zeros_like(new_token)
    for t in range(tokens):
        new_depth = jnp.where(new_token == t, depth_ref[t], new_depth)
    own_depth = jnp.zeros_like(own_token)
    for t in range(share):
        own_depth = jnp.where(own_token == t, depth_ref[first + t], own_depth)
    seen = (new_depth <= own_depth) & (new_kv == own_kv)
    query = query_ref[pl.ds(first, share)].reshape(per, head_dim)
    scores = dot_rows(query, keys_ref[...]) * score_scale + jnp.where(seen, 0.0, DEAD)
    peak, total, weighted = softmax_parts(scores, values_ref[...])
    out_ref[:per, :] = weighted
    stats = stat_lanes(peak, total, head_dim)
    row = lax.broadcasted_iota(jnp.int32, (WIDE_ROWS, LANES), 0)
    for at in range(per // LANES):
        turned = dot_rows(eye(STAT_ROWS, head_dim), stats[at * LANES : (at + 1) * LANES])
        peaks = turned[0:1] + turned[1:2] + turned[2:3]
        totals = turned[3:4] + turned[4:5] + turned[5:6]
        start = per + at * WIDE_ROWS
        out_ref[start : start + WIDE_ROWS, :] = jnp.where(row == 0, peaks, totals)


def fresh_rows(query, new_keys, new_values, depth, score_scale, ways):
    tokens, heads, head_dim = query.shape
    per = tokens * heads // ways
    flat = (new_keys.shape[0] * new_keys.shape[1], head_dim)
    inputs = [
        pltpu.with_memory_space_constraint(x, pltpu.HBM)
        for x in (new_keys.reshape(flat), new_values.reshape(flat), depth)
    ]
    return pl.pallas_call(
        functools.partial(fresh_kernel, score_scale, ways),
        out_shape=jax.ShapeDtypeStruct((per + per // LANES * WIDE_ROWS, head_dim), F32),
        in_specs=[VMEM, HBM, HBM, HBM],
        out_specs=VMEM,
        scratch_shapes=[
            pltpu.VMEM(flat, BF16),
            pltpu.VMEM(flat, BF16),
            pltpu.SMEM(depth.shape, jnp.int32),
            pltpu.SemaphoreType.DMA((3,)),
        ],
        compiler_params=PARAMS,
        name="fresh",
    )(query, *inputs)


def tree(combine, parts):
    while len(parts) > 1:
        pairs = [combine(parts[k], parts[k + 1]) for k in range(0, len(parts) - 1, 2)]
        parts = pairs + parts[len(parts) & ~1 :]
    return parts[0]


def merge_kernel(per, last, *refs):
    *in_refs, out_ref = refs
    head_dim = out_ref.shape[1]
    chunks = per // LANES
    turn = eye(LANES, LANES)
    factor_rows = -(-3 * len(in_refs) // STAT_ROWS) * STAT_ROWS
    for at in range(chunks):
        peaks, totals = [], []
        for ref in in_refs:
            rows_in = (ref.shape[0] - per) // chunks
            stats = ref[per + at * rows_in : per + (at + 1) * rows_in, :].astype(F32)
            if ref.dtype == BF16:
                peaks.append(stats[0:1] + stats[1:2] + stats[2:3])
                totals.append(stats[3:4] + stats[4:5] + stats[5:6])
            else:
                peaks.append(stats[0:1])
                totals.append(stats[1:2])
        peak = tree(jnp.maximum, peaks)
        factors = [jnp.exp(p - peak) for p in peaks]
        total = tree(jnp.add, [f * t for f, t in zip(factors, totals)])
        if last:
            factors = [f / total for f in factors]
        else:
            start = per + at * WIDE_ROWS
            row = lax.broadcasted_iota(jnp.int32, (WIDE_ROWS, LANES), 0)
            out_ref[start : start + WIDE_ROWS, :] = jnp.where(row == 0, peak, total)
        parts = [part for f in factors for part in three_parts(f)]
        columns = dot_rows(turn, stacked(parts, (factor_rows, LANES)))
        terms = []
        for k, ref in enumerate(in_refs):
            column = columns[:, 3 * k : 3 * k + 1] + columns[:, 3 * k + 1 : 3 * k + 2]
            column = jnp.broadcast_to(column + columns[:, 3 * k + 2 : 3 * k + 3], (LANES, head_dim))
            terms.append(ref[at * LANES : (at + 1) * LANES, :].astype(F32) * column)
        out_ref[at * LANES : (at + 1) * LANES, :] = tree(jnp.add, terms).astype(out_ref.dtype)


def merge(states, per, last):
    head_dim = states[0].shape[1]
    if last:
        out = jax.ShapeDtypeStruct((per, head_dim), BF16)
    else:
        out = jax.ShapeDtypeStruct((per + per // LANES * WIDE_ROWS, head_dim), F32)
    return pl.pallas_call(
        functools.partial(merge_kernel, per, last),
        out_shape=out,
        in_specs=[VMEM] * len(states),
        out_specs=VMEM,
        compiler_params=PARAMS,
        name="merge",
    )(*states)


def join_kernel(*refs):
    *in_refs, out_ref, sems = refs
    ways = len(in_refs)
    per = in_refs[0].shape[0]
    here = place_of(lax.axis_index("seq"), ways)
    copies = []
    for way, ref in enumerate(in_refs):
        start = pl.multiple_of(lax.bitwise_xor(here, way) * per, per)
        copies.append(pltpu.make_async_copy(ref, out_ref.at[pl.ds(start, per)], sems.at[way]))
        copies[-1].start()
    for copy in copies:
        copy.wait()


def join(pieces):
    per, head_dim = pieces[0].shape
    return pl.pallas_call(
        join_kernel,
        out_shape=jax.ShapeDtypeStruct((len(pieces) * per, head_dim), BF16),
        in_specs=[VMEM] * len(pieces),
        out_specs=HBM,
        scratch_shapes=[pltpu.SemaphoreType.DMA((len(pieces),))],
        compiler_params=PARAMS,
        name="join",
    )(*pieces)


def relay_kernel(kv_count, slots_hbm, length_ref, got_ref, keys_ref, values_ref, slots_ref, sem):
    copy = pltpu.make_async_copy(slots_hbm, slots_ref, sem)
    copy.start()
    copy.wait()
    slot_count, span, head_dim = keys_ref.shape
    row = lax.broadcasted_iota(jnp.int32, (span, head_dim), 0)
    live = length_ref[0] * kv_count - lax.axis_index("seq") * (slot_count * span)

    def one(t, carry):
        slot = slots_ref[t]
        kept = row < live - t * span
        for c, out_ref in enumerate((keys_ref, values_ref)):
            block = got_ref[slot // 2, c, slot % 2].astype(F32)
            out_ref[t] = jnp.where(kept, block, 0.0).astype(BF16)
        return carry

    lax.fori_loop(0, slot_count, one, 0, unroll=4)


def relay(span_slots, prompt_length, got, kv_count):
    _, _, _, span, head_dim = got.shape
    shape = jax.ShapeDtypeStruct((span_slots.shape[0], span, head_dim), BF16)
    return pl.pallas_call(
        functools.partial(relay_kernel, kv_count),
        out_shape=(shape, shape),
        in_specs=[HBM, SMEM, VMEM],
        out_specs=(VMEM, VMEM),
        scratch_shapes=[pltpu.SMEM(span_slots.shape, jnp.int32), pltpu.SemaphoreType.DMA],
        compiler_params=PARAMS,
        name="relay",
    )(pltpu.with_memory_space_constraint(span_slots, pltpu.HBM), prompt_length, got)


def step(
    cache_keys,
    cache_values,
    span_slots,
    prompt_length,
    queries,
    new_keys,
    new_values,
    decode_offsets,
):
    row_count, kv_all, head_dim = cache_keys.shape
    seq_count = lax.axis_size("seq")
    head_count = lax.axis_size("head")
    cycle_size = seq_count * head_count
    slot_count = span_slots.shape[0]
    span_rows = row_count // (2 * seq_count)
    kv_local = kv_all // head_count
    token_count, heads, _ = queries.shape
    score_scale = 1.0 / math.sqrt(head_dim)
    shard_rows = slot_count * span_rows
    ways = math.gcd(4, seq_count)

    packed, mine, away, place, query = pack(
        cache_keys, cache_values, span_slots, queries, seq_count, head_count
    )
    flat = (2, row_count * kv_local, head_dim)
    blocks = [mine.reshape(flat)]
    for shift in range(1, head_count):
        blocks.append(
            lax.ppermute(
                away[shift - 1].reshape(flat),
                "head",
                [(h, (h + shift) % head_count) for h in range(head_count)],
            )
        )
    got = lax.all_to_all(
        packed.reshape(cycle_size, 2, 2 * span_rows * kv_local, head_dim),
        ("head", "seq"),
        split_axis=0,
        concat_axis=0,
        tiled=True,
    )

    pieces = attend(prompt_length, query, place, blocks, score_scale, ways)
    per = token_count * heads // ways

    def swapped(x, distance):
        return lax.ppermute(x, "seq", [(s, s ^ distance) for s in range(seq_count)])

    states = [pieces[0]]
    for way in range(1, ways):
        states.append(swapped(pieces[way], way))
    fresh = fresh_rows(query, new_keys, new_values, decode_offsets, score_scale, ways)
    distance = ways
    while distance < seq_count:
        state = merge(states, per, False)
        states = [state, swapped(state, hop_distance(distance, ways))]
        distance *= 2
    state = merge(states + [fresh], per, True)
    finished = [state]
    for way in range(1, ways):
        finished.append(swapped(state, way))
    attended = join(finished)

    relaid_keys, relaid_values = relay(
        span_slots,
        prompt_length,
        got.reshape(cycle_size, 2, 2, span_rows * kv_local, head_dim),
        kv_local,
    )
    whole = (shard_rows, kv_local, head_dim)
    return (
        relaid_keys.reshape(whole),
        relaid_values.reshape(whole),
        attended.reshape(token_count, heads, head_dim),
    )


def solution(mesh):
    return jax.shard_map(
        step,
        mesh=mesh,
        in_specs=(
            P(("rep", "head", "seq"), None, None),
            P(("rep", "head", "seq"), None, None),
            P("rep"),
            P("rep"),
            P("rep", "head", None),
            P("rep", "head", None),
            P("rep", "head", None),
            P("rep"),
        ),
        out_specs=(
            P(("rep", "seq"), "head", None),
            P(("rep", "seq"), "head", None),
            P("rep", "head", None),
        ),
        check_vma=False,
    )
```

```python
import functools
import math

import jax
import jax.numpy as jnp
from jax import lax
from jax.experimental import pallas as pl
from jax.experimental.pallas import tpu as pltpu
from jax.sharding import PartitionSpec as P


BF16 = jnp.bfloat16
F32 = jnp.float32
DEAD = -1e30
STAT_ROWS = 8
WIDE_ROWS = 8
LANES = 128
VMEM = pl.BlockSpec(memory_space=pltpu.VMEM)
SMEM = pl.BlockSpec(memory_space=pltpu.SMEM)
HBM = pl.BlockSpec(memory_space=pltpu.HBM)
PARAMS = pltpu.CompilerParams(vmem_limit_bytes=16 * 1024 * 1024)


def dot_rows(a, b):
    return lax.dot_general(a, b, (((1,), (1,)), ((), ())), preferred_element_type=F32)


def three_parts(x):
    high = x.astype(BF16).astype(F32)
    rest = x - high
    middle = rest.astype(BF16).astype(F32)
    return [high, middle, rest - middle]


def stacked(parts, like):
    row = lax.broadcasted_iota(jnp.int32, like, 0)
    out = jnp.zeros(like, F32)
    for at, part in enumerate(parts):
        out = jnp.where(row == at, part, out)
    return out.astype(BF16)


def eye(rows, columns):
    return (
        lax.broadcasted_iota(jnp.int32, (rows, columns), 0)
        == lax.broadcasted_iota(jnp.int32, (rows, columns), 1)
    ).astype(F32).astype(BF16)


def split_off(x, n):
    if n & (n - 1) == 0:
        return x & (n - 1), x >> (n.bit_length() - 1)
    return lax.rem(x, n), lax.div(x, n)


def place_of(index, ways):
    return lax.rem(lax.bitwise_xor(index, lax.div(lax.rem(index, 2 * ways), ways) * (ways // 2)), ways)


def hop_distance(distance, ways):
    return distance + ways // 2 if distance == ways else distance


def pack_kernel(
    span_rows,
    keys_ref,
    values_ref,
    slots_hbm,
    query_hbm,
    send_ref,
    mine_ref,
    away_ref,
    place_ref,
    query_ref,
    slots_ref,
    in_sems,
    out_sems,
    sems,
):
    seq_count, _, head_count, _, _ = keys_ref.shape
    slot_count = slots_hbm.shape[0]
    me = lax.axis_index("head")
    seq_index = lax.axis_index("seq")
    facts = pltpu.make_async_copy(slots_hbm, slots_ref, sems.at[0])
    facts.start()
    staged = pltpu.make_async_copy(query_hbm, query_ref, sems.at[1])
    blocks = []
    for shift in list(range(1, head_count)) + [0]:
        h = lax.rem(me + shift, head_count)
        for c, source in enumerate((keys_ref, values_ref)):
            target = away_ref.at[shift - 1, c] if shift else mine_ref.at[c]
            copy = pltpu.make_async_copy(source.at[:, :, h], target, in_sems.at[shift, c])
            copy.start()
            out = pltpu.make_async_copy(target, send_ref.at[h, :, c], out_sems.at[shift, c])
            blocks.append((copy, out))
    staged.start()
    for copy, out in blocks:
        copy.wait()
        out.start()
    facts.wait()

    wanted = []
    for b in range(head_count):
        first = 2 * (lax.rem(me + head_count - b, head_count) * seq_count + seq_index)
        wanted += [first, first + 1]

    def look(t, places):
        slot = slots_ref[t]
        return tuple(jnp.where(slot == w, t, p) for w, p in zip(wanted, places))

    places = lax.fori_loop(0, slot_count, look, tuple(jnp.int32(0) for _ in wanted))
    column = lax.broadcasted_iota(jnp.int32, (1, place_ref.shape[1]), 1)
    row, rest = split_off(column, span_rows)
    half, rest = split_off(rest, 2)
    turn, block = split_off(rest, seq_count)
    span = jnp.zeros_like(column)
    for at, place in enumerate(places):
        span = jnp.where(2 * block + half == at, place, span)
    place_ref[...] = (turn * slot_count + span) * span_rows + row
    for _, out in blocks:
        out.wait()
    staged.wait()


def pack(cache_keys, cache_values, span_slots, queries, seq_count, head_count):
    row_count, kv_all, head_dim = cache_keys.shape
    kv = kv_all // head_count
    rows = row_count // seq_count
    split = (seq_count, rows, head_count, kv, head_dim)
    block = (seq_count, rows, kv, head_dim)
    inputs = [
        pltpu.with_memory_space_constraint(x, pltpu.HBM)
        for x in (cache_keys.reshape(split), cache_values.reshape(split), span_slots, queries)
    ]
    return pl.pallas_call(
        functools.partial(pack_kernel, rows // 2),
        out_shape=(
            jax.ShapeDtypeStruct((head_count, seq_count, 2, rows, kv, head_dim), BF16),
            jax.ShapeDtypeStruct((2,) + block, BF16),
            jax.ShapeDtypeStruct((head_count - 1, 2) + block, BF16),
            jax.ShapeDtypeStruct((1, head_count * row_count), jnp.int32),
            jax.ShapeDtypeStruct(queries.shape, BF16),
        ),
        in_specs=[HBM] * len(inputs),
        out_specs=(HBM,) + (VMEM,) * 4,
        scratch_shapes=[
            pltpu.SMEM(span_slots.shape, jnp.int32),
            pltpu.SemaphoreType.DMA((head_count, 2)),
            pltpu.SemaphoreType.DMA((head_count, 2)),
            pltpu.SemaphoreType.DMA((2,)),
        ],
        compiler_params=PARAMS,
        name="pack",
    )(*inputs)


def softmax_parts(scores, values):
    peak = jnp.max(scores, axis=1, keepdims=True)
    weights = jnp.exp(scores - peak)
    total = jnp.sum(weights, axis=1, keepdims=True)
    high = weights.astype(BF16)
    low = (weights - high.astype(F32)).astype(BF16)
    weighted = jnp.dot(
        jnp.concatenate([high, low], axis=1),
        jnp.concatenate([values, values], axis=0),
        preferred_element_type=F32,
    )
    return peak, total, weighted


def stat_lanes(peak, total, head_dim):
    lane = lax.broadcasted_iota(jnp.int32, (peak.shape[0], head_dim), 1)
    stats = jnp.zeros((peak.shape[0], head_dim), F32)
    for at, part in enumerate(three_parts(peak) + three_parts(total)):
        stats = jnp.where(lane == at, part, stats)
    return stats.astype(BF16)


def attend_kernel(score_scale, ways, length_ref, query_ref, place_ref, *rest):
    *block_refs, rows_buf, stat_buf, wide_buf = rest
    block_refs, out_refs = block_refs[:-ways], block_refs[-ways:]
    tokens, heads, head_dim = query_ref.shape
    kv_count = rows_buf.shape[1]
    group = heads // kv_count
    stored = block_refs[0].shape[1]
    for at, ref in enumerate(block_refs):
        for c in range(2):
            wide_buf[c, at * stored : (at + 1) * stored, :] = ref[c].astype(F32)
    columns = place_ref.shape[1]
    bias = jnp.where(place_ref[...] < length_ref[0], 0.0, DEAD)
    for g in range(kv_count):
        query = query_ref[:, g * group : (g + 1) * group, :].reshape(tokens * group, head_dim)
        own = pl.ds(g, columns, stride=kv_count)
        keys = wide_buf[0, own, :].astype(BF16)
        values = wide_buf[1, own, :].astype(BF16)
        peak, total, weighted = softmax_parts(dot_rows(query, keys) * score_scale + bias, values)
        rows_buf[:, g] = weighted.astype(BF16).reshape(tokens, group, head_dim)
        stat_buf[:, g] = stat_lanes(peak, total, head_dim).reshape(tokens, group, head_dim)
    here = place_of(lax.axis_index("seq"), ways)
    share = tokens // ways
    per = share * heads
    pick = eye(STAT_ROWS, head_dim)
    for way, out_ref in enumerate(out_refs):
        first = lax.bitwise_xor(here, way) * share
        out_ref[:per, :] = rows_buf[pl.ds(first, share)].reshape(per, head_dim)
        turned = dot_rows(pick, stat_buf[pl.ds(first, share)].reshape(per, head_dim)).astype(BF16)
        for at in range(per // LANES):
            start = per + at * STAT_ROWS
            out_ref[start : start + STAT_ROWS, :] = turned[:, at * LANES : (at + 1) * LANES]


def attend(length, query, place, blocks, score_scale, ways):
    tokens, heads, head_dim = query.shape
    rows = sum(block.shape[1] for block in blocks)
    kv_count = rows // place.shape[1]
    group = heads // kv_count
    per = tokens * heads // ways
    piece = jax.ShapeDtypeStruct((per + per // LANES * STAT_ROWS, head_dim), BF16)
    return pl.pallas_call(
        functools.partial(attend_kernel, score_scale, ways),
        out_shape=(piece,) * ways,
        in_specs=[SMEM] + [VMEM] * (2 + len(blocks)),
        out_specs=(VMEM,) * ways,
        scratch_shapes=[
            pltpu.VMEM((tokens, kv_count, group, head_dim), BF16),
            pltpu.VMEM((tokens, kv_count, group, head_dim), BF16),
            pltpu.VMEM((2, rows, head_dim), F32),
        ],
        compiler_params=PARAMS,
        name="attend",
    )(length, query, place, *blocks)


def fresh_kernel(
    score_scale, ways, query_ref, keys_hbm, values_hbm, depth_hbm, out_ref, keys_ref, values_ref, depth_ref, sems
):
    copies = [
        pltpu.make_async_copy(source, target, sems.at[at])
        for at, (source, target) in enumerate(
            ((keys_hbm, keys_ref), (values_hbm, values_ref), (depth_hbm, depth_ref))
        )
    ]
    for copy in copies:
        copy.start()
    tokens, heads, head_dim = query_ref.shape
    kv_count = keys_ref.shape[0] // tokens
    share = tokens // ways
    per = share * heads
    first = place_of(lax.axis_index("seq"), ways) * share
    shape = (per, tokens * kv_count)
    _, own = split_off(lax.broadcasted_iota(jnp.int32, shape, 0), heads // kv_count)
    own_kv, own_token = split_off(own, kv_count)
    new_kv, new_token = split_off(lax.broadcasted_iota(jnp.int32, (1, shape[1]), 1), kv_count)
    for copy in copies:
        copy.wait()
    new_depth = jnp.zeros_like(new_token)
    for t in range(tokens):
        new_depth = jnp.where(new_token == t, depth_ref[t], new_depth)
    own_depth = jnp.zeros_like(own_token)
    for t in range(share):
        own_depth = jnp.where(own_token == t, depth_ref[first + t], own_depth)
    seen = (new_depth <= own_depth) & (new_kv == own_kv)
    query = query_ref[pl.ds(first, share)].reshape(per, head_dim)
    scores = dot_rows(query, keys_ref[...]) * score_scale + jnp.where(seen, 0.0, DEAD)
    peak, total, weighted = softmax_parts(scores, values_ref[...])
    out_ref[:per, :] = weighted
    stats = stat_lanes(peak, total, head_dim)
    row = lax.broadcasted_iota(jnp.int32, (WIDE_ROWS, LANES), 0)
    for at in range(per // LANES):
        turned = dot_rows(eye(STAT_ROWS, head_dim), stats[at * LANES : (at + 1) * LANES])
        peaks = turned[0:1] + turned[1:2] + turned[2:3]
        totals = turned[3:4] + turned[4:5] + turned[5:6]
        start = per + at * WIDE_ROWS
        out_ref[start : start + WIDE_ROWS, :] = jnp.where(row == 0, peaks, totals)


def fresh_rows(query, new_keys, new_values, depth, score_scale, ways):
    tokens, heads, head_dim = query.shape
    per = tokens * heads // ways
    flat = (new_keys.shape[0] * new_keys.shape[1], head_dim)
    inputs = [
        pltpu.with_memory_space_constraint(x, pltpu.HBM)
        for x in (new_keys.reshape(flat), new_values.reshape(flat), depth)
    ]
    return pl.pallas_call(
        functools.partial(fresh_kernel, score_scale, ways),
        out_shape=jax.ShapeDtypeStruct((per + per // LANES * WIDE_ROWS, head_dim), F32),
        in_specs=[VMEM, HBM, HBM, HBM],
        out_specs=VMEM,
        scratch_shapes=[
            pltpu.VMEM(flat, BF16),
            pltpu.VMEM(flat, BF16),
            pltpu.SMEM(depth.shape, jnp.int32),
            pltpu.SemaphoreType.DMA((3,)),
        ],
        compiler_params=PARAMS,
        name="fresh",
    )(query, *inputs)


def tree(combine, parts):
    while len(parts) > 1:
        pairs = [combine(parts[k], parts[k + 1]) for k in range(0, len(parts) - 1, 2)]
        parts = pairs + parts[len(parts) & ~1 :]
    return parts[0]


def merge_kernel(per, last, *refs):
    *in_refs, out_ref = refs
    head_dim = out_ref.shape[1]
    chunks = per // LANES
    turn = eye(LANES, LANES)
    factor_rows = -(-3 * len(in_refs) // STAT_ROWS) * STAT_ROWS
    for at in range(chunks):
        peaks, totals = [], []
        for ref in in_refs:
            rows_in = (ref.shape[0] - per) // chunks
            stats = ref[per + at * rows_in : per + (at + 1) * rows_in, :].astype(F32)
            if ref.dtype == BF16:
                peaks.append(stats[0:1] + stats[1:2] + stats[2:3])
                totals.append(stats[3:4] + stats[4:5] + stats[5:6])
            else:
                peaks.append(stats[0:1])
                totals.append(stats[1:2])
        peak = tree(jnp.maximum, peaks)
        factors = [jnp.exp(p - peak) for p in peaks]
        total = tree(jnp.add, [f * t for f, t in zip(factors, totals)])
        if last:
            factors = [f / total for f in factors]
        else:
            start = per + at * WIDE_ROWS
            row = lax.broadcasted_iota(jnp.int32, (WIDE_ROWS, LANES), 0)
            out_ref[start : start + WIDE_ROWS, :] = jnp.where(row == 0, peak, total)
        parts = [part for f in factors for part in three_parts(f)]
        columns = dot_rows(turn, stacked(parts, (factor_rows, LANES)))
        terms = []
        for k, ref in enumerate(in_refs):
            column = columns[:, 3 * k : 3 * k + 1] + columns[:, 3 * k + 1 : 3 * k + 2]
            column = jnp.broadcast_to(column + columns[:, 3 * k + 2 : 3 * k + 3], (LANES, head_dim))
            terms.append(ref[at * LANES : (at + 1) * LANES, :].astype(F32) * column)
        out_ref[at * LANES : (at + 1) * LANES, :] = tree(jnp.add, terms).astype(out_ref.dtype)


def merge(states, per, last):
    head_dim = states[0].shape[1]
    if last:
        out = jax.ShapeDtypeStruct((per, head_dim), BF16)
    else:
        out = jax.ShapeDtypeStruct((per + per // LANES * WIDE_ROWS, head_dim), F32)
    return pl.pallas_call(
        functools.partial(merge_kernel, per, last),
        out_shape=out,
        in_specs=[VMEM] * len(states),
        out_specs=VMEM,
        compiler_params=PARAMS,
        name="merge",
    )(*states)


def join_kernel(*refs):
    *in_refs, out_ref, sems = refs
    ways = len(in_refs)
    per = in_refs[0].shape[0]
    here = place_of(lax.axis_index("seq"), ways)
    copies = []
    for way, ref in enumerate(in_refs):
        start = pl.multiple_of(lax.bitwise_xor(here, way) * per, per)
        copies.append(pltpu.make_async_copy(ref, out_ref.at[pl.ds(start, per)], sems.at[way]))
        copies[-1].start()
    for copy in copies:
        copy.wait()


def join(pieces):
    per, head_dim = pieces[0].shape
    return pl.pallas_call(
        join_kernel,
        out_shape=jax.ShapeDtypeStruct((len(pieces) * per, head_dim), BF16),
        in_specs=[VMEM] * len(pieces),
        out_specs=HBM,
        scratch_shapes=[pltpu.SemaphoreType.DMA((len(pieces),))],
        compiler_params=PARAMS,
        name="join",
    )(*pieces)


def relay_kernel(kv_count, slots_hbm, length_ref, got_ref, keys_ref, values_ref, slots_ref, sem):
    copy = pltpu.make_async_copy(slots_hbm, slots_ref, sem)
    copy.start()
    copy.wait()
    slot_count, span, head_dim = keys_ref.shape
    row = lax.broadcasted_iota(jnp.int32, (span, head_dim), 0)
    live = length_ref[0] * kv_count - lax.axis_index("seq") * (slot_count * span)

    def one(t, carry):
        slot = slots_ref[t]
        kept = row < live - t * span
        for c, out_ref in enumerate((keys_ref, values_ref)):
            block = got_ref[slot // 2, c, slot % 2].astype(F32)
            out_ref[t] = jnp.where(kept, block, 0.0).astype(BF16)
        return carry

    lax.fori_loop(0, slot_count, one, 0, unroll=4)


def relay(span_slots, prompt_length, got, kv_count):
    _, _, _, span, head_dim = got.shape
    shape = jax.ShapeDtypeStruct((span_slots.shape[0], span, head_dim), BF16)
    return pl.pallas_call(
        functools.partial(relay_kernel, kv_count),
        out_shape=(shape, shape),
        in_specs=[HBM, SMEM, VMEM],
        out_specs=(VMEM, VMEM),
        scratch_shapes=[pltpu.SMEM(span_slots.shape, jnp.int32), pltpu.SemaphoreType.DMA],
        compiler_params=PARAMS,
        name="relay",
    )(pltpu.with_memory_space_constraint(span_slots, pltpu.HBM), prompt_length, got)


def step(
    cache_keys,
    cache_values,
    span_slots,
    prompt_length,
    queries,
    new_keys,
    new_values,
    decode_offsets,
):
    row_count, kv_all, head_dim = cache_keys.shape
    seq_count = lax.axis_size("seq")
    head_count = lax.axis_size("head")
    cycle_size = seq_count * head_count
    slot_count = span_slots.shape[0]
    span_rows = row_count // (2 * seq_count)
    kv_local = kv_all // head_count
    token_count, heads, _ = queries.shape
    score_scale = 1.0 / math.sqrt(head_dim)
    shard_rows = slot_count * span_rows
    ways = math.gcd(4, seq_count)

    packed, mine, away, place, query = pack(
        cache_keys, cache_values, span_slots, queries, seq_count, head_count
    )
    flat = (2, row_count * kv_local, head_dim)
    blocks = [mine.reshape(flat)]
    for shift in range(1, head_count):
        blocks.append(
            lax.ppermute(
                away[shift - 1].reshape(flat),
                "head",
                [(h, (h + shift) % head_count) for h in range(head_count)],
            )
        )
    got = lax.all_to_all(
        packed.reshape(cycle_size, 2, 2 * span_rows * kv_local, head_dim),
        ("head", "seq"),
        split_axis=0,
        concat_axis=0,
        tiled=True,
    )

    pieces = attend(prompt_length, query, place, blocks, score_scale, ways)
    per = token_count * heads // ways

    def swapped(x, distance):
        return lax.ppermute(x, "seq", [(s, s ^ distance) for s in range(seq_count)])

    states = [pieces[0]]
    for way in range(1, ways):
        states.append(swapped(pieces[way], way))
    fresh = fresh_rows(query, new_keys, new_values, decode_offsets, score_scale, ways)
    distance = ways
    while distance < seq_count:
        state = merge(states, per, False)
        states = [state, swapped(state, hop_distance(distance, ways))]
        distance *= 2
    state = merge(states + [fresh], per, True)
    finished = [state]
    for way in range(1, ways):
        finished.append(swapped(state, way))
    attended = join(finished)

    relaid_keys, relaid_values = relay(
        span_slots,
        prompt_length,
        got.reshape(cycle_size, 2, 2, span_rows * kv_local, head_dim),
        kv_local,
    )
    whole = (shard_rows, kv_local, head_dim)
    return (
        relaid_keys.reshape(whole),
        relaid_values.reshape(whole),
        attended.reshape(token_count, heads, head_dim),
    )


def solution(mesh):
    return jax.shard_map(
        step,
        mesh=mesh,
        in_specs=(
            P(("rep", "head", "seq"), None, None),
            P(("rep", "head", "seq"), None, None),
            P("rep"),
            P("rep"),
            P("rep", "head", None),
            P("rep", "head", None),
            P("rep", "head", None),
            P("rep"),
        ),
        out_specs=(
            P(("rep", "seq"), "head", None),
            P(("rep", "seq"), "head", None),
            P("rep", "head", None),
        ),
        check_vma=False,
    )
```
